32 devices in a mesh: clip: 4 (over y, core), seq: 4 (over z), help: 2 (over x).
Axes of the slice: x: 2, y: 2, z: 4, core: 2. Of those that a mesh axis runs over, the one named last changes fastest.
Arguments:
- query_states: bfloat16 [4096, 2048], P(('clip', 'seq', 'help')), parts along dimension 0, may hold values from -8 to 8
- key_states: bfloat16 [4096, 2048], P(('clip', 'seq', 'help')), parts along dimension 0, may hold values from -8 to 8
- value_states: bfloat16 [4096, 2048], P(('clip', 'seq', 'help')), parts along dimension 0, may hold values from -6 to 6
- tile_lists: int32 [64, 8, 2], P('clip'), parts along dimension 0, may hold values from 0 to 7, as said below
- tile_counts: int32 [64, 8], P('clip'), parts along dimension 0, may hold values from 1 to 2, as said below
Outputs:
- attended: bfloat16 [4096, 2048], P(('clip', 'seq', 'help')), parts along dimension 0
The draws below stay inside these ranges and needn't reach their ends.
There are 4 independent parts, one for each index of `clip`. The reference program is written for one: setup_inputs(seed, part) draws one part's arguments, and reference() takes and returns one part's arrays. A program takes and returns all parts, laid end to end along the dimension named above; each array names one. Nothing has to cross between parts.
Inputs may be any that keep to these rules, and one draw needn't show every extreme that they name: tile_lists[h, t, :] holds 2 different key tiles, the first of which is t itself; the entries at slots tile_counts[h, t] and beyond are ignored. `tile_counts`: in every head some query tile has count 2.
All inputs are finite; a program needn't handle non-finite values.
Results may differ from the reference program's by a relative error of at most 0.0044.
Values may be sent and summed in bfloat16 or wider, within the bound.
No kernel may reach another device: no remote copies, remote signals or barrier semaphores. Data moves between devices by JAX's collectives and lax.ppermute only.
A program may use at most 64 MiB of HBM per device.

```python
import jax
import jax.numpy as jnp
from jax import lax

H = 16
DH = 128
TILE = 128
SEQ_LEN = 1024
QT = 8
SLOTS = 2
D = 2048


def tile_plan(key):
    base = jax.random.fold_in(key, 4242)
    heavy_key, raw_key, place_key, order_key = jax.random.split(base, 4)
    heavy = jax.random.randint(heavy_key, (H, QT), 0, 4) == 0
    ceiling = jnp.where(heavy, SLOTS, max(SLOTS // 4, 1))
    raw_counts = jax.random.randint(raw_key, (H, QT), 0, QT)
    counts = 1 + raw_counts % ceiling
    forced_tile = jax.random.randint(place_key, (H, 1), 0, QT)
    tile_index = jnp.arange(QT, dtype=jnp.int32)[None, :]
    counts = jnp.where(tile_index == forced_tile, SLOTS, counts).astype(jnp.int32)
    ranking = jax.random.randint(order_key, (H, QT, QT), 0, 1 << 20) * QT
    ranking = ranking + jnp.arange(QT, dtype=jnp.int32)[None, None, :]
    own_tile = jnp.arange(QT, dtype=jnp.int32)[:, None] == jnp.arange(QT, dtype=jnp.int32)[None, :]
    ranking = jnp.where(own_tile[None, :, :], -1, ranking)
    lists = jnp.argsort(ranking, axis=-1)[:, :, :SLOTS].astype(jnp.int32)
    return (lists, counts)


def draw_tile_lists(key, part):
    return tile_plan(key)[0]


def draw_tile_counts(key, part):
    return tile_plan(key)[1]


def draw_query_states(key, part):
    own_key = jax.random.fold_in(key, 1)
    states = jax.random.normal(own_key, (SEQ_LEN, D), jnp.float32)
    return jnp.clip(states, -8.0, 8.0).astype(jnp.bfloat16)


def draw_key_states(key, part):
    own_key = jax.random.fold_in(key, 2)
    states = jax.random.normal(own_key, (SEQ_LEN, D), jnp.float32)
    return jnp.clip(states, -8.0, 8.0).astype(jnp.bfloat16)


def level_of(key, shape, pieces, least, top_value):
    loudness, own = 1.0, jax.random.fold_in(key, 6)
    for dim, blocks in pieces:
        steps = jnp.exp(jax.random.uniform(jax.random.fold_in(own, dim), (blocks,), jnp.float32, least / len(pieces), top_value / len(pieces)))
        loudness = loudness * jnp.repeat(steps, shape[dim] // blocks).reshape([-1 if axis == dim else 1 for axis in range(len(shape))])
    return loudness


def normal_values(rng, shape, spread, reach, cuts=(), kind=jnp.bfloat16):
    entries = jax.random.normal(rng, shape, jnp.float32) * spread
    if len(cuts) > 0:
        entries = level_of(rng, shape, cuts, -0.22, 0.18) * entries
    return jnp.clip(entries, min=-reach, max=reach).astype(kind)


def setup_inputs(seed: int = 0, part: int = 0) -> dict:
    key_of = jax.random.split(jax.random.key(seed), 6)
    part_splits = jax.random.split(jax.random.fold_in(key_of[5], part), 6)
    query_states = draw_query_states(jax.random.fold_in(jax.random.fold_in(key_of[5], part), 71), part)
    key_states = draw_key_states(jax.random.fold_in(jax.random.fold_in(key_of[5], part), 71), part)
    value_states = normal_values(part_splits[2], (SEQ_LEN, D), 1.0, 6.0, ((0, 8),))
    tile_lists = draw_tile_lists(jax.random.fold_in(jax.random.fold_in(key_of[5], part), 71), part)
    tile_counts = draw_tile_counts(jax.random.fold_in(jax.random.fold_in(key_of[5], part), 71), part)
    return {"query_states": query_states, "key_states": key_states, "value_states": value_states, "tile_lists": tile_lists, "tile_counts": tile_counts}


big_negative = -1e30


def attend_tiles(query_tiles, key_tiles, value_tiles, tile_lists, tile_counts):
    row_tiles, tile_rows, head_width = query_tiles.shape
    factor = head_width ** -0.5
    query_float = query_tiles.astype(jnp.float32)
    start_state = (jnp.full((row_tiles, tile_rows, 1), big_negative, jnp.float32),
                   jnp.zeros((row_tiles, tile_rows, 1), jnp.float32),
                   jnp.zeros((row_tiles, tile_rows, head_width), jnp.float32))

    def one_slot(slot_index, carried):
        running_max, running_sum, weighted = carried
        chosen = lax.dynamic_index_in_dim(tile_lists, slot_index, axis=1, keepdims=False)
        key_block = jnp.take(key_tiles, chosen, axis=0).astype(jnp.float32)
        value_block = jnp.take(value_tiles, chosen, axis=0).astype(jnp.float32)
        scores = jnp.einsum("qtd,qsd->qts", query_float, key_block) * factor
        new_max = jnp.maximum(running_max, jnp.max(scores, axis=2, keepdims=True))
        shrink = jnp.exp(running_max - new_max)
        tile_weights = jnp.exp(scores - new_max)
        new_sum = running_sum * shrink + jnp.sum(tile_weights, axis=2, keepdims=True)
        rounded = lax.optimization_barrier(tile_weights.astype(jnp.bfloat16)).astype(jnp.float32)
        new_weighted = weighted * shrink + jnp.einsum("qts,qsd->qtd", rounded, value_block)
        live = (slot_index < tile_counts)[:, None, None]
        return (jnp.where(live, new_max, running_max),
                jnp.where(live, new_sum, running_sum),
                jnp.where(live, new_weighted, weighted))

    final_state = lax.fori_loop(0, jnp.max(tile_counts), one_slot, start_state)
    return (final_state[2] / final_state[1]).astype(jnp.bfloat16)


def reference(query_states, key_states, value_states, tile_lists, tile_counts):
    seq_total, model_width = query_states.shape
    tile_total = seq_total // TILE

    def by_head(states):
        return states.reshape(tile_total, TILE, H, DH).transpose(2, 0, 1, 3)

    attended = lax.map(lambda packed: attend_tiles(*packed),
                       (by_head(query_states), by_head(key_states), by_head(value_states), tile_lists, tile_counts))
    return attended.transpose(1, 2, 0, 3).reshape(seq_total, model_width)
```

```python
import jax
import jax.numpy as jnp
from jax import lax
from jax.experimental import pallas as pl
from jax.experimental.pallas import tpu as pltpu
from jax.sharding import PartitionSpec as P

H = 16
DH = 128
TILE = 128
ROUND = 4


big_negative = -1e30


def pick_tiles(table, index):
    table_rows = table.shape[0]
    selector = (index[:, None] == jnp.arange(table_rows, dtype=jnp.int32)[None, :]).astype(
        jnp.bfloat16
    )
    picked = jnp.dot(selector, table.reshape(table_rows, -1), preferred_element_type=jnp.float32)
    return picked.astype(jnp.bfloat16).reshape((index.shape[0],) + table.shape[1:])


def attend_items(query_items, key_tiles, value_tiles, item_lists, item_counts):
    item_total, tile_rows, head_width = query_items.shape
    factor = head_width ** (-0.5)
    batches = item_total // ROUND
    joined = jnp.concatenate((key_tiles, value_tiles), axis=2)

    def one_batch(packed):
        queries, lists, counts = packed
        start_state = (
            jnp.full((ROUND, tile_rows, 1), big_negative, jnp.float32),
            jnp.zeros((ROUND, tile_rows, 1), jnp.float32),
            jnp.zeros((ROUND, tile_rows, head_width), jnp.float32),
        )

        def one_slot(slot_index, carried):
            running_max, running_sum, weighted = carried
            chosen = lax.dynamic_index_in_dim(lists, slot_index, axis=1, keepdims=False)
            both_blocks = pick_tiles(joined, chosen)
            key_block = both_blocks[:, :, :head_width]
            value_block = both_blocks[:, :, head_width:]
            scores = (
                jnp.einsum("qtd,qsd->qts", queries, key_block, preferred_element_type=jnp.float32)
                * factor
            )
            new_max = jnp.maximum(running_max, jnp.max(scores, axis=2, keepdims=True))
            shrink = jnp.exp(running_max - new_max)
            tile_weights = jnp.exp(scores - new_max)
            new_sum = running_sum * shrink + jnp.sum(tile_weights, axis=2, keepdims=True)
            new_weighted = weighted * shrink + jnp.einsum(
                "qts,qsd->qtd",
                tile_weights.astype(jnp.bfloat16),
                value_block,
                preferred_element_type=jnp.float32,
            )
            live = (slot_index < counts)[:, None, None]
            return (
                jnp.where(live, new_max, running_max),
                jnp.where(live, new_sum, running_sum),
                jnp.where(live, new_weighted, weighted),
            )

        final_state = lax.fori_loop(0, jnp.max(counts), one_slot, start_state)
        return (final_state[2] / final_state[1]).astype(jnp.bfloat16)

    finished = lax.map(
        one_batch,
        (
            query_items.reshape(batches, ROUND, tile_rows, head_width),
            item_lists.reshape(batches, ROUND, item_lists.shape[1]),
            item_counts.reshape(batches, ROUND),
        ),
    )
    return finished.reshape(item_total, tile_rows, head_width)


def shards_by_seq(query_states, key_states, value_states, tile_lists, tile_counts):
    groups = lax.axis_size("seq")
    helpers = lax.axis_size("help")
    device = lax.axis_index("seq")
    helper = lax.axis_index("help")
    row_count = query_states.shape[0]
    heads_here = H // groups
    head_cols = heads_here * DH
    tile_total = tile_lists.shape[1]
    per_block = row_count // TILE
    owned_total = groups * per_block

    def to_groups(states):
        return states.reshape(row_count, groups, head_cols)

    arrived = (
        lax.all_to_all(to_groups(query_states), "seq", split_axis=1, concat_axis=0, tiled=True),
        lax.all_to_all(to_groups(key_states), "seq", split_axis=1, concat_axis=0, tiled=True),
        lax.all_to_all(to_groups(value_states), "seq", split_axis=1, concat_axis=0, tiled=True),
    )
    arrived_query = arrived[0].reshape(groups, 1, row_count, head_cols)
    arrived_key = arrived[1].reshape(groups, 1, row_count, head_cols)
    arrived_value = arrived[2].reshape(groups, 1, row_count, head_cols)
    head_lists = lax.dynamic_slice_in_dim(tile_lists, device * heads_here, heads_here, 0)
    head_counts = lax.dynamic_slice_in_dim(tile_counts, device * heads_here, heads_here, 0)
    head_offset = (jnp.arange(heads_here, dtype=jnp.int32) * tile_total)[:, None, None]
    flat_lists = (head_lists + head_offset).reshape(heads_here * tile_total, head_lists.shape[2])
    flat_counts = head_counts.reshape(heads_here * tile_total)

    def head_tiles(whole):
        shaped = whole.reshape(tile_total, TILE, heads_here, DH).transpose(2, 0, 1, 3)
        return shaped.reshape(heads_here * tile_total, TILE, DH)

    key_whole, value_whole = (
        lax.all_gather(arrived_key, "help", axis=1, tiled=True),
        lax.all_gather(arrived_value, "help", axis=1, tiled=True),
    )
    key_tiles = head_tiles(key_whole)
    value_tiles = head_tiles(value_whole)
    own_tiles = arrived_query.reshape(owned_total, TILE, heads_here, DH).transpose(2, 0, 1, 3)
    own_tiles = own_tiles.reshape(heads_here * owned_total, TILE, DH)
    local_index = jnp.arange(owned_total, dtype=jnp.int32)
    global_tile = (
        local_index // per_block * helpers + helper
    ) * per_block + local_index % per_block
    item_index = (
        jnp.arange(heads_here, dtype=jnp.int32)[:, None] * tile_total + global_tile[None, :]
    )
    item_index = item_index.reshape(heads_here * owned_total)
    results = attend_items(
        own_tiles,
        key_tiles,
        value_tiles,
        jnp.take(flat_lists, item_index, axis=0),
        jnp.take(flat_counts, item_index, axis=0),
    )
    owned = results.reshape(heads_here, owned_total, TILE, DH)
    leaving = owned.transpose(1, 2, 0, 3)
    leaving = leaving.reshape(groups, row_count, head_cols)
    returned = lax.all_to_all(leaving, "seq", split_axis=0, concat_axis=2, tiled=True)
    return returned.reshape(row_count, H * DH)


GROUP = ("seq", "help")
VMEM = pl.BlockSpec(memory_space=pltpu.VMEM)
SMEM = pl.BlockSpec(memory_space=pltpu.SMEM)


def pack_kernel(key_ref, value_ref, out_ref):
    owners, _, width = out_ref.shape
    half = width // 2
    for owner in range(owners):
        cols = slice(owner * half, (owner + 1) * half)
        out_ref[owner, :, :half] = key_ref[:, cols]
        out_ref[owner, :, half:] = value_ref[:, cols]


def pick_kernel(lists_ref, held_ref, out_ref):
    tiles, _, width = out_ref.shape
    heads = width // (2 * DH)
    first = (lax.axis_index("seq") * lax.axis_size("help") + lax.axis_index("help")) * heads
    for tile in range(tiles):
        for head in range(heads):
            chosen = lists_ref[first + head, tile]
            for base in (0, width // 2):
                cols = slice(base + head * DH, base + (head + 1) * DH)
                out_ref[tile, :, cols] = held_ref[chosen, :, cols]


def dot_t(a, b):
    return lax.dot_general(a, b, (((1,), (1,)), ((), ())), preferred_element_type=jnp.float32)


def attend_kernel(counts_ref, query_ref, key_ref, value_ref, far_ref, out_ref):
    head_total = query_ref.shape[1] // DH
    owners, _, width = far_ref.shape
    heads = head_total // owners
    tile = lax.axis_index("seq") * lax.axis_size("help") + lax.axis_index("help")
    factor = DH ** (-0.5)
    for head in range(head_total):
        cols = slice(head * DH, (head + 1) * DH)
        owner, inner = head // heads, head % heads
        far_key = far_ref[owner, :, inner * DH : (inner + 1) * DH]
        far_value = far_ref[owner, :, width // 2 + inner * DH : width // 2 + (inner + 1) * DH]
        query = query_ref[:, cols]
        near = dot_t(query, key_ref[:, cols]) * factor
        near_max = jnp.max(near, axis=1, keepdims=True)
        near_p = jnp.exp(near - near_max)
        near_sum = jnp.sum(near_p, axis=1, keepdims=True)
        near_out = jnp.dot(
            near_p.astype(jnp.bfloat16), value_ref[:, cols], preferred_element_type=jnp.float32
        )
        live = counts_ref[head, tile] > 1
        far = jnp.where(live, dot_t(query, far_key) * factor, big_negative)
        both_max = jnp.maximum(near_max, jnp.max(far, axis=1, keepdims=True))
        shrink = jnp.exp(near_max - both_max)
        far_p = jnp.where(live, jnp.exp(far - both_max), 0.0)
        total = near_sum * shrink + jnp.sum(far_p, axis=1, keepdims=True)
        weighted = near_out * shrink + jnp.dot(
            far_p.astype(jnp.bfloat16), far_value, preferred_element_type=jnp.float32
        )
        out_ref[:, cols] = (weighted / total).astype(out_ref.dtype)


def shards_by_device(query_states, key_states, value_states, tile_lists, tile_counts):
    rows, width = query_states.shape
    owners = lax.axis_size(GROUP)
    block = jax.ShapeDtypeStruct((owners, rows, 2 * width // owners), key_states.dtype)
    packed = pl.pallas_call(
        pack_kernel, out_shape=block, in_specs=[VMEM, VMEM], out_specs=VMEM, name="pack"
    )(key_states, value_states)
    held = lax.all_to_all(packed, GROUP, split_axis=0, concat_axis=0, tiled=True)
    picked = pl.pallas_call(
        pick_kernel, out_shape=block, in_specs=[SMEM, VMEM], out_specs=VMEM, name="pick"
    )(tile_lists[:, :, 1], held)
    far = lax.all_to_all(picked, GROUP, split_axis=0, concat_axis=0, tiled=True)
    return pl.pallas_call(
        attend_kernel,
        out_shape=jax.ShapeDtypeStruct((rows, width), query_states.dtype),
        in_specs=[SMEM, VMEM, VMEM, VMEM, VMEM],
        out_specs=VMEM,
        name="attend",
    )(tile_counts, query_states, key_states, value_states, far)


def shards(query_states, key_states, value_states, tile_lists, tile_counts):
    rows = query_states.shape[0]
    head_total, tile_total, slots = tile_lists.shape
    owners = lax.axis_size("seq") * lax.axis_size("help")
    one_tile = rows == TILE and tile_total == owners
    if one_tile and slots == 2 and head_total % owners == 0:
        return shards_by_device(query_states, key_states, value_states, tile_lists, tile_counts)
    return shards_by_seq(query_states, key_states, value_states, tile_lists, tile_counts)


def solution(mesh):
    placed = (
        P(("clip", "seq", "help"), None),
        P(("clip", "seq", "help"), None),
        P(("clip", "seq", "help"), None),
        P("clip", None, None),
        P("clip", None),
    )
    return jax.shard_map(
        shards,
        mesh=mesh,
        in_specs=placed,
        out_specs=P(("clip", "seq", "help"), None),
        check_vma=False,
    )
```

```python
import math

import jax
import jax.numpy as jnp
from jax import lax
from jax.experimental import pallas as pl
from jax.experimental.pallas import tpu as pltpu
from jax.sharding import PartitionSpec as P

H = 16
DH = 128
TILE = 128
ROUND = 4


big_negative = -1e30


def pick_tiles(table, index):
    table_rows = table.shape[0]
    selector = (index[:, None] == jnp.arange(table_rows, dtype=jnp.int32)[None, :]).astype(
        jnp.bfloat16
    )
    picked = jnp.dot(selector, table.reshape(table_rows, -1), preferred_element_type=jnp.float32)
    return picked.astype(jnp.bfloat16).reshape((index.shape[0],) + table.shape[1:])


def attend_items(query_items, key_tiles, value_tiles, item_lists, item_counts):
    item_total, tile_rows, head_width = query_items.shape
    factor = head_width ** (-0.5)
    batches = item_total // ROUND
    joined = jnp.concatenate((key_tiles, value_tiles), axis=2)

    def one_batch(packed):
        queries, lists, counts = packed
        start_state = (
            jnp.full((ROUND, tile_rows, 1), big_negative, jnp.float32),
            jnp.zeros((ROUND, tile_rows, 1), jnp.float32),
            jnp.zeros((ROUND, tile_rows, head_width), jnp.float32),
        )

        def one_slot(slot_index, carried):
            running_max, running_sum, weighted = carried
            chosen = lax.dynamic_index_in_dim(lists, slot_index, axis=1, keepdims=False)
            both_blocks = pick_tiles(joined, chosen)
            key_block = both_blocks[:, :, :head_width]
            value_block = both_blocks[:, :, head_width:]
            scores = (
                jnp.einsum("qtd,qsd->qts", queries, key_block, preferred_element_type=jnp.float32)
                * factor
            )
            new_max = jnp.maximum(running_max, jnp.max(scores, axis=2, keepdims=True))
            shrink = jnp.exp(running_max - new_max)
            tile_weights = jnp.exp(scores - new_max)
            new_sum = running_sum * shrink + jnp.sum(tile_weights, axis=2, keepdims=True)
            new_weighted = weighted * shrink + jnp.einsum(
                "qts,qsd->qtd",
                tile_weights.astype(jnp.bfloat16),
                value_block,
                preferred_element_type=jnp.float32,
            )
            live = (slot_index < counts)[:, None, None]
            return (
                jnp.where(live, new_max, running_max),
                jnp.where(live, new_sum, running_sum),
                jnp.where(live, new_weighted, weighted),
            )

        final_state = lax.fori_loop(0, jnp.max(counts), one_slot, start_state)
        return (final_state[2] / final_state[1]).astype(jnp.bfloat16)

    finished = lax.map(
        one_batch,
        (
            query_items.reshape(batches, ROUND, tile_rows, head_width),
            item_lists.reshape(batches, ROUND, item_lists.shape[1]),
            item_counts.reshape(batches, ROUND),
        ),
    )
    return finished.reshape(item_total, tile_rows, head_width)


def shards_by_seq(query_states, key_states, value_states, tile_lists, tile_counts):
    groups = lax.axis_size("seq")
    helpers = lax.axis_size("help")
    device = lax.axis_index("seq")
    helper = lax.axis_index("help")
    row_count = query_states.shape[0]
    heads_here = H // groups
    head_cols = heads_here * DH
    tile_total = tile_lists.shape[1]
    per_block = row_count // TILE
    owned_total = groups * per_block

    def to_groups(states):
        return states.reshape(row_count, groups, head_cols)

    arrived = (
        lax.all_to_all(to_groups(query_states), "seq", split_axis=1, concat_axis=0, tiled=True),
        lax.all_to_all(to_groups(key_states), "seq", split_axis=1, concat_axis=0, tiled=True),
        lax.all_to_all(to_groups(value_states), "seq", split_axis=1, concat_axis=0, tiled=True),
    )
    arrived_query = arrived[0].reshape(groups, 1, row_count, head_cols)
    arrived_key = arrived[1].reshape(groups, 1, row_count, head_cols)
    arrived_value = arrived[2].reshape(groups, 1, row_count, head_cols)
    head_lists = lax.dynamic_slice_in_dim(tile_lists, device * heads_here, heads_here, 0)
    head_counts = lax.dynamic_slice_in_dim(tile_counts, device * heads_here, heads_here, 0)
    head_offset = (jnp.arange(heads_here, dtype=jnp.int32) * tile_total)[:, None, None]
    flat_lists = (head_lists + head_offset).reshape(heads_here * tile_total, head_lists.shape[2])
    flat_counts = head_counts.reshape(heads_here * tile_total)

    def head_tiles(whole):
        shaped = whole.reshape(tile_total, TILE, heads_here, DH).transpose(2, 0, 1, 3)
        return shaped.reshape(heads_here * tile_total, TILE, DH)

    key_whole, value_whole = (
        lax.all_gather(arrived_key, "help", axis=1, tiled=True),
        lax.all_gather(arrived_value, "help", axis=1, tiled=True),
    )
    key_tiles = head_tiles(key_whole)
    value_tiles = head_tiles(value_whole)
    own_tiles = arrived_query.reshape(owned_total, TILE, heads_here, DH).transpose(2, 0, 1, 3)
    own_tiles = own_tiles.reshape(heads_here * owned_total, TILE, DH)
    local_index = jnp.arange(owned_total, dtype=jnp.int32)
    global_tile = (
        local_index // per_block * helpers + helper
    ) * per_block + local_index % per_block
    item_index = (
        jnp.arange(heads_here, dtype=jnp.int32)[:, None] * tile_total + global_tile[None, :]
    )
    item_index = item_index.reshape(heads_here * owned_total)
    results = attend_items(
        own_tiles,
        key_tiles,
        value_tiles,
        jnp.take(flat_lists, item_index, axis=0),
        jnp.take(flat_counts, item_index, axis=0),
    )
    owned = results.reshape(heads_here, owned_total, TILE, DH)
    leaving = owned.transpose(1, 2, 0, 3)
    leaving = leaving.reshape(groups, row_count, head_cols)
    returned = lax.all_to_all(leaving, "seq", split_axis=0, concat_axis=2, tiled=True)
    return returned.reshape(row_count, H * DH)


GROUP = ("seq", "help")
ANY = pl.BlockSpec(memory_space=pl.ANY)
VMEM = pl.BlockSpec(memory_space=pltpu.VMEM)
PARAMS = pltpu.CompilerParams(vmem_limit_bytes=12 << 20)
STAGGER_NS = 0


def position():
    return lax.axis_index("seq") * lax.axis_size("help") + lax.axis_index("help")


def pack_kernel(key_ref, value_ref, out_ref, sems):
    owners, parts = out_ref.shape[:2]
    reads = []
    for owner in range(owners):
        for part in range(parts):
            source = (key_ref, value_ref)[part % 2]
            head = owner * (parts // 2) + part // 2
            reads.append(
                pltpu.make_async_copy(
                    source.at[:, head * DH : (head + 1) * DH],
                    out_ref.at[owner, part],
                    sems.at[owner * parts + part],
                )
            )
            reads[-1].start()
    if STAGGER_NS:
        @pl.when(lax.axis_index("clip") % 2 == 1)
        def _():
            pl.delay(STAGGER_NS)

    for read in reads:
        read.wait()


def index_bits(tiles):
    return (tiles - 1).bit_length()


def pick_kernel(lists_ref, held_ref, out_ref):
    tiles, parts = out_ref.shape[:2]
    heads = parts // 2
    bits = index_bits(tiles)
    first = position() * heads
    listed = lists_ref[:, 1, :]
    of_head = lax.broadcasted_iota(jnp.int32, listed.shape, 1)
    of_tile = lax.broadcasted_iota(jnp.int32, listed.shape, 0)
    placed = listed << (bits * of_tile)
    for head in range(heads):
        own = jnp.where(of_head == first + head, placed, 0).astype(jnp.float32)
        joined = jnp.sum(own).astype(jnp.int32)
        pair = slice(2 * head, 2 * head + 2)
        for tile in range(tiles):
            chosen = (joined >> (bits * tile)) & ((1 << bits) - 1)
            out_ref[tile, pair] = held_ref[chosen, pair]


def attend_kernel(counts_ref, query_ref, key_ref, value_ref, far_ref, out_ref, scores, weights):
    rows, width = query_ref.shape
    inner = far_ref.shape[1] // 2
    factor = DH ** (-0.5) * math.log2(math.e)
    heads = range(width // DH)
    for head in heads:
        cols = slice(head * DH, (head + 1) * DH)
        far_key = far_ref[head // inner, 2 * (head % inner)]
        scores[head] = lax.dot_general(
            query_ref[:, cols],
            jnp.concatenate((key_ref[:, cols], far_key), axis=0),
            (((1,), (1,)), ((), ())),
            preferred_element_type=jnp.float32,
        )
    counts = counts_ref[pl.ds(position(), 1), :]
    square = (counts.shape[1], counts.shape[1])
    own = lax.broadcasted_iota(jnp.int32, square, 0) == lax.broadcasted_iota(jnp.int32, square, 1)
    used = jnp.sum(jnp.where(own, counts, 0).astype(jnp.float32), axis=1, keepdims=True) > 1.5
    masks = jnp.where(jnp.broadcast_to(used, (square[0], TILE)), 0.0, big_negative)
    for head in heads:
        near = scores[head, :, :TILE]
        far = scores[head, :, TILE:] + masks[head : head + 1]
        top = jnp.max(jnp.maximum(near, far), axis=1, keepdims=True)
        weights[head, :, :TILE] = jnp.exp2((near - top) * factor).astype(weights.dtype)
        weights[head, :, TILE:] = jnp.exp2((far - top) * factor).astype(weights.dtype)
    for head in heads:
        cols = slice(head * DH, (head + 1) * DH)
        far_value = far_ref[head // inner, 2 * (head % inner) + 1]
        value = jnp.concatenate((value_ref[:, cols], far_value), axis=0)
        widened = jnp.concatenate((value, jnp.ones_like(value)), axis=1)
        product = jnp.dot(weights[head], widened, preferred_element_type=jnp.float32)
        out_ref[:, cols] = (product[:, :DH] / product[:, DH:]).astype(out_ref.dtype)


def shards_by_device(query_states, key_states, value_states, tile_lists, tile_counts):
    rows, width = query_states.shape
    owners = lax.axis_size(GROUP)
    parts = 2 * width // DH // owners
    block = jax.ShapeDtypeStruct((owners, parts, rows, DH), key_states.dtype)
    packed = pl.pallas_call(
        pack_kernel,
        out_shape=block,
        in_specs=[ANY, ANY],
        out_specs=VMEM,
        scratch_shapes=[pltpu.SemaphoreType.DMA((owners * parts,))],
        compiler_params=PARAMS,
        name="pack",
    )(*(pltpu.with_memory_space_constraint(x, pltpu.HBM) for x in (key_states, value_states)))
    held = lax.all_to_all(packed, GROUP, split_axis=0, concat_axis=0, tiled=True)
    picked = pl.pallas_call(
        pick_kernel,
        out_shape=block,
        in_specs=[VMEM, VMEM],
        out_specs=VMEM,
        compiler_params=PARAMS,
        name="pick",
    )(tile_lists.transpose(1, 2, 0), held)
    far = lax.all_to_all(picked, GROUP, split_axis=0, concat_axis=0, tiled=True)
    return pl.pallas_call(
        attend_kernel,
        out_shape=jax.ShapeDtypeStruct((rows, width), query_states.dtype),
        in_specs=[VMEM] * 5,
        out_specs=VMEM,
        scratch_shapes=[
            pltpu.VMEM((width // DH, rows, 2 * TILE), jnp.float32),
            pltpu.VMEM((width // DH, rows, 2 * TILE), jnp.bfloat16),
        ],
        compiler_params=PARAMS,
        name="attend",
    )(tile_counts.T, query_states, key_states, value_states, far)


def shards(query_states, key_states, value_states, tile_lists, tile_counts):
    rows = query_states.shape[0]
    head_total, tile_total, slots = tile_lists.shape
    owners = lax.axis_size(GROUP)
    one_tile = rows == TILE and tile_total == owners
    joins = tile_total * index_bits(tile_total) <= 24
    if one_tile and joins and slots == 2 and head_total % owners == 0:
        return shards_by_device(query_states, key_states, value_states, tile_lists, tile_counts)
    return shards_by_seq(query_states, key_states, value_states, tile_lists, tile_counts)


def solution(mesh):
    placed = (
        P(("clip", "seq", "help"), None),
        P(("clip", "seq", "help"), None),
        P(("clip", "seq", "help"), None),
        P("clip", None, None),
        P("clip", None),
    )
    return jax.shard_map(
        shards,
        mesh=mesh,
        in_specs=placed,
        out_specs=P(("clip", "seq", "help"), None),
        check_vma=False,
    )
```

```python
import math

import jax
import jax.numpy as jnp
from jax import lax
from jax.experimental import pallas as pl
from jax.experimental.pallas import tpu as pltpu
from jax.sharding import PartitionSpec as P

H = 16
DH = 128
TILE = 128
ROUND = 4


big_negative = -1e30


def pick_tiles(table, index):
    table_rows = table.shape[0]
    selector = (index[:, None] == jnp.arange(table_rows, dtype=jnp.int32)[None, :]).astype(
        jnp.bfloat16
    )
    picked = jnp.dot(selector, table.reshape(table_rows, -1), preferred_element_type=jnp.float32)
    return picked.astype(jnp.bfloat16).reshape((index.shape[0],) + table.shape[1:])


def attend_items(query_items, key_tiles, value_tiles, item_lists, item_counts):
    item_total, tile_rows, head_width = query_items.shape
    factor = head_width ** (-0.5)
    batches = item_total // ROUND
    joined = jnp.concatenate((key_tiles, value_tiles), axis=2)

    def one_batch(packed):
        queries, lists, counts = packed
        start_state = (
            jnp.full((ROUND, tile_rows, 1), big_negative, jnp.float32),
            jnp.zeros((ROUND, tile_rows, 1), jnp.float32),
            jnp.zeros((ROUND, tile_rows, head_width), jnp.float32),
        )

        def one_slot(slot_index, carried):
            running_max, running_sum, weighted = carried
            chosen = lax.dynamic_index_in_dim(lists, slot_index, axis=1, keepdims=False)
            both_blocks = pick_tiles(joined, chosen)
            key_block = both_blocks[:, :, :head_width]
            value_block = both_blocks[:, :, head_width:]
            scores = (
                jnp.einsum("qtd,qsd->qts", queries, key_block, preferred_element_type=jnp.float32)
                * factor
            )
            new_max = jnp.maximum(running_max, jnp.max(scores, axis=2, keepdims=True))
            shrink = jnp.exp(running_max - new_max)
            tile_weights = jnp.exp(scores - new_max)
            new_sum = running_sum * shrink + jnp.sum(tile_weights, axis=2, keepdims=True)
            new_weighted = weighted * shrink + jnp.einsum(
                "qts,qsd->qtd",
                tile_weights.astype(jnp.bfloat16),
                value_block,
                preferred_element_type=jnp.float32,
            )
            live = (slot_index < counts)[:, None, None]
            return (
                jnp.where(live, new_max, running_max),
                jnp.where(live, new_sum, running_sum),
                jnp.where(live, new_weighted, weighted),
            )

        final_state = lax.fori_loop(0, jnp.max(counts), one_slot, start_state)
        return (final_state[2] / final_state[1]).astype(jnp.bfloat16)

    finished = lax.map(
        one_batch,
        (
            query_items.reshape(batches, ROUND, tile_rows, head_width),
            item_lists.reshape(batches, ROUND, item_lists.shape[1]),
            item_counts.reshape(batches, ROUND),
        ),
    )
    return finished.reshape(item_total, tile_rows, head_width)


def shards_by_seq(query_states, key_states, value_states, tile_lists, tile_counts):
    groups = lax.axis_size("seq")
    helpers = lax.axis_size("help")
    device = lax.axis_index("seq")
    helper = lax.axis_index("help")
    row_count = query_states.shape[0]
    heads_here = H // groups
    head_cols = heads_here * DH
    tile_total = tile_lists.shape[1]
    per_block = row_count // TILE
    owned_total = groups * per_block

    def to_groups(states):
        return states.reshape(row_count, groups, head_cols)

    arrived = (
        lax.all_to_all(to_groups(query_states), "seq", split_axis=1, concat_axis=0, tiled=True),
        lax.all_to_all(to_groups(key_states), "seq", split_axis=1, concat_axis=0, tiled=True),
        lax.all_to_all(to_groups(value_states), "seq", split_axis=1, concat_axis=0, tiled=True),
    )
    arrived_query = arrived[0].reshape(groups, 1, row_count, head_cols)
    arrived_key = arrived[1].reshape(groups, 1, row_count, head_cols)
    arrived_value = arrived[2].reshape(groups, 1, row_count, head_cols)
    head_lists = lax.dynamic_slice_in_dim(tile_lists, device * heads_here, heads_here, 0)
    head_counts = lax.dynamic_slice_in_dim(tile_counts, device * heads_here, heads_here, 0)
    head_offset = (jnp.arange(heads_here, dtype=jnp.int32) * tile_total)[:, None, None]
    flat_lists = (head_lists + head_offset).reshape(heads_here * tile_total, head_lists.shape[2])
    flat_counts = head_counts.reshape(heads_here * tile_total)

    def head_tiles(whole):
        shaped = whole.reshape(tile_total, TILE, heads_here, DH).transpose(2, 0, 1, 3)
        return shaped.reshape(heads_here * tile_total, TILE, DH)

    key_whole, value_whole = (
        lax.all_gather(arrived_key, "help", axis=1, tiled=True),
        lax.all_gather(arrived_value, "help", axis=1, tiled=True),
    )
    key_tiles = head_tiles(key_whole)
    value_tiles = head_tiles(value_whole)
    own_tiles = arrived_query.reshape(owned_total, TILE, heads_here, DH).transpose(2, 0, 1, 3)
    own_tiles = own_tiles.reshape(heads_here * owned_total, TILE, DH)
    local_index = jnp.arange(owned_total, dtype=jnp.int32)
    global_tile = (
        local_index // per_block * helpers + helper
    ) * per_block + local_index % per_block
    item_index = (
        jnp.arange(heads_here, dtype=jnp.int32)[:, None] * tile_total + global_tile[None, :]
    )
    item_index = item_index.reshape(heads_here * owned_total)
    results = attend_items(
        own_tiles,
        key_tiles,
        value_tiles,
        jnp.take(flat_lists, item_index, axis=0),
        jnp.take(flat_counts, item_index, axis=0),
    )
    owned = results.reshape(heads_here, owned_total, TILE, DH)
    leaving = owned.transpose(1, 2, 0, 3)
    leaving = leaving.reshape(groups, row_count, head_cols)
    returned = lax.all_to_all(leaving, "seq", split_axis=0, concat_axis=2, tiled=True)
    return returned.reshape(row_count, H * DH)


GROUP = ("seq", "help")
ANY = pl.BlockSpec(memory_space=pl.ANY)
VMEM = pl.BlockSpec(memory_space=pltpu.VMEM)
PARAMS = pltpu.CompilerParams(vmem_limit_bytes=12 << 20)
STAGGER_NS = 0


def position():
    return lax.axis_index("seq") * lax.axis_size("help") + lax.axis_index("help")


def pack_kernel(key_ref, value_ref, out_ref, sems):
    owners, parts = out_ref.shape[:2]
    reads = []
    for owner in range(owners):
        for part in range(parts):
            source = (key_ref, value_ref)[part % 2]
            head = owner * (parts // 2) + part // 2
            reads.append(
                pltpu.make_async_copy(
                    source.at[:, head * DH : (head + 1) * DH],
                    out_ref.at[owner, part],
                    sems.at[owner * parts + part],
                )
            )
            reads[-1].start()
    if STAGGER_NS:
        @pl.when(lax.axis_index("clip") % 2 == 1)
        def _():
            pl.delay(STAGGER_NS)

    for read in reads:
        read.wait()


def index_bits(tiles):
    return (tiles - 1).bit_length()


def pick_kernel(lists_ref, held_ref, out_ref):
    tiles, parts = out_ref.shape[:2]
    heads = parts // 2
    bits = index_bits(tiles)
    first = position() * heads
    listed = lists_ref[:, 1, :]
    of_head = lax.broadcasted_iota(jnp.int32, listed.shape, 1)
    of_tile = lax.broadcasted_iota(jnp.int32, listed.shape, 0)
    placed = listed << (bits * of_tile)
    for head in range(heads):
        own = jnp.where(of_head == first + head, placed, 0).astype(jnp.float32)
        joined = jnp.sum(own).astype(jnp.int32)
        pair = slice(2 * head, 2 * head + 2)
        for tile in range(tiles):
            chosen = (joined >> (bits * tile)) & ((1 << bits) - 1)
            out_ref[tile, pair] = held_ref[chosen, pair]


def attend(counts_ref, query_ref, key, value, far_key, far_value, out_ref, scores, weights):
    width = query_ref.shape[1]
    factor = DH ** (-0.5) * math.log2(math.e)
    heads = range(width // DH)
    for head in heads:
        scores[head] = lax.dot_general(
            query_ref[:, head * DH : (head + 1) * DH],
            jnp.concatenate((key(head), far_key(head)), axis=0),
            (((1,), (1,)), ((), ())),
            preferred_element_type=jnp.float32,
        )
    counts = counts_ref[pl.ds(position(), 1), :]
    square = (counts.shape[1], counts.shape[1])
    own = lax.broadcasted_iota(jnp.int32, square, 0) == lax.broadcasted_iota(jnp.int32, square, 1)
    used = jnp.sum(jnp.where(own, counts, 0).astype(jnp.float32), axis=1, keepdims=True) > 1.5
    masks = jnp.where(jnp.broadcast_to(used, (square[0], TILE)), 0.0, big_negative)
    for head in heads:
        near = scores[head, :, :TILE]
        far = scores[head, :, TILE:] + masks[head : head + 1]
        top = jnp.max(jnp.maximum(near, far), axis=1, keepdims=True)
        weights[head, :, :TILE] = jnp.exp2((near - top) * factor).astype(weights.dtype)
        weights[head, :, TILE:] = jnp.exp2((far - top) * factor).astype(weights.dtype)
    for head in heads:
        values = jnp.concatenate((value(head), far_value(head)), axis=0)
        widened = jnp.concatenate((values, jnp.ones_like(values)), axis=1)
        product = jnp.dot(weights[head], widened, preferred_element_type=jnp.float32)
        out_ref[:, head * DH : (head + 1) * DH] = (product[:, :DH] / product[:, DH:]).astype(
            out_ref.dtype
        )


def attend_scratch(rows, width):
    shape = (width // DH, rows, 2 * TILE)
    return [pltpu.VMEM(shape, jnp.float32), pltpu.VMEM(shape, jnp.bfloat16)]


def shards_by_owner(query_states, key_states, value_states, tile_lists, tile_counts):
    rows, width = query_states.shape
    owners = lax.axis_size(GROUP)
    parts = 2 * width // DH // owners
    block = jax.ShapeDtypeStruct((owners, parts, rows, DH), key_states.dtype)
    packed = pl.pallas_call(
        pack_kernel,
        out_shape=block,
        in_specs=[ANY, ANY],
        out_specs=VMEM,
        scratch_shapes=[pltpu.SemaphoreType.DMA((owners * parts,))],
        compiler_params=PARAMS,
        name="pack",
    )(*(pltpu.with_memory_space_constraint(x, pltpu.HBM) for x in (key_states, value_states)))
    held = lax.all_to_all(packed, GROUP, split_axis=0, concat_axis=0, tiled=True)
    picked = pl.pallas_call(
        pick_kernel,
        out_shape=block,
        in_specs=[VMEM, VMEM],
        out_specs=VMEM,
        compiler_params=PARAMS,
        name="pick",
    )(tile_lists.transpose(1, 2, 0), held)
    far = lax.all_to_all(picked, GROUP, split_axis=0, concat_axis=0, tiled=True)
    return pl.pallas_call(
        attend_by_owner_kernel,
        out_shape=jax.ShapeDtypeStruct((rows, width), query_states.dtype),
        in_specs=[VMEM] * 5,
        out_specs=VMEM,
        scratch_shapes=attend_scratch(rows, width),
        compiler_params=PARAMS,
        name="attend",
    )(tile_counts.T, query_states, key_states, value_states, far)


def plan_kernel(
    lists_ref, counts_ref, key_ref, value_ref, send_ref, own_ref, route_ref, fail_ref, sems
):
    tiles, head_total = counts_ref.shape
    reads = []
    for head in range(head_total):
        for which, source in enumerate((key_ref, value_ref)):
            reads.append(
                pltpu.make_async_copy(
                    source.at[:, head * DH : (head + 1) * DH],
                    own_ref.at[head, which],
                    sems.at[2 * head + which],
                )
            )
            reads[-1].start()

    me = position()
    shape = (tiles, head_total)
    of_tile = lax.broadcasted_iota(jnp.int32, shape, 0)
    of_head = lax.broadcasted_iota(jnp.int32, shape, 1)
    source = lists_ref[:, 1, :]
    wanted = counts_ref[...] > 1
    code = jnp.where(wanted, source, -1)
    rank = jnp.zeros(shape, jnp.int32)
    for head in range(head_total - 1):
        same = (code[:, head : head + 1] == source) & (of_head > head)
        rank = rank + same.astype(jnp.int32)
    first = wanted & (rank == 0)
    second = wanted & (rank == 1)
    further = wanted & (rank > 1)

    def along(block):
        total = jnp.sum(block.astype(jnp.float32), axis=1, keepdims=True)
        return jnp.broadcast_to(total.astype(jnp.int32), shape)

    def only(block):
        total = jnp.sum(jnp.sum(block.astype(jnp.float32), axis=1, keepdims=True), axis=0, keepdims=True)
        return jnp.broadcast_to(total.astype(jnp.int32), shape)

    def least(block):
        least_f = jnp.min(jnp.min(block.astype(jnp.float32), axis=1, keepdims=True), axis=0, keepdims=True)
        return jnp.broadcast_to(least_f.astype(jnp.int32), shape)

    bit = jnp.int32(1) << source
    mine = source == me
    none = 1 << 20
    state = (
        jnp.where(further, of_tile * head_total + of_head, none),
        first.astype(jnp.int32),
        along(jnp.where(first, bit, 0)),
        along(jnp.where(first, bit, 0)),
        along(jnp.where(second, bit, 0)),
        along(jnp.where(first & mine, of_head, 0)),
        along(jnp.where(second & mine, of_head, 0)),
        jnp.where(first, source, jnp.where(second, tiles + source, 0)),
        jnp.zeros(shape, jnp.int32),
    )

    def relay(_, state):
        key, direct, held1, movable, held2, send1, send2, where, fail = state
        here = key == least(key)
        to = only(jnp.where(here, of_tile, 0))
        head = only(jnp.where(here, of_head, 0))
        start = only(jnp.where(here, source, 0))
        held2_to = only(jnp.where((of_tile == to) & (of_head == 0), held2, 0))
        used1 = (held1 >> start) & 1
        fixed = 1 - ((movable >> start) & 1) * (1 - ((held2 >> start) & 1))
        free = ((held2_to >> of_tile) & 1) == 0
        free = free & (of_tile != start) & (of_tile != to) & ((used1 == 0) | (fixed == 0))
        best = least(jnp.where(free, of_tile + tiles * used1, none))
        good = best < none
        moved = good & (best >= tiles)
        via = jnp.where(moved, best - tiles, best)
        at_via = good & (of_tile == via)
        at_to = good & (of_tile == to)
        shifted = at_via & moved & (direct > 0) & (source == start)
        where = jnp.where(shifted, tiles + start, where)
        where = jnp.where(here & good, tiles + via, where)
        direct = jnp.where(shifted, 0, direct)
        send2 = jnp.where(at_via & moved & (start == me), send1, send2)
        send1 = jnp.where(at_via & (start == me), head, send1)
        send2 = jnp.where(at_to & (via == me), head_total + start, send2)
        start_bit = jnp.int32(1) << start
        held1 = jnp.where(at_via, held1 | start_bit, held1)
        movable = jnp.where(at_via, movable & ~start_bit, movable)
        held2 = jnp.where(at_via & moved, held2 | start_bit, held2)
        held2 = jnp.where(at_to, held2 | (jnp.int32(1) << jnp.where(good, via, 0)), held2)
        fail = jnp.where(good, fail, 1)
        key = jnp.where(here, none, key)
        return key, direct, held1, movable, held2, send1, send2, where, fail

    relays = jnp.sum(further.astype(jnp.float32)).astype(jnp.int32)
    state = lax.fori_loop(0, relays, relay, state)
    send1, send2, where, fail = state[5:]
    route_ref[0] = send2
    route_ref[1] = where
    fail_ref[...] = fail
    sent = [pick_one(send1, of_tile == tile) for tile in range(tiles)]
    for read in reads:
        read.wait()
    for tile in range(tiles):
        send_ref[tile] = own_ref[sent[tile]]


def pick_one(block, at):
    return jnp.max(jnp.where(at, block, 0).astype(jnp.float32)).astype(jnp.int32)


def forward_kernel(route_ref, own_ref, got_ref, send_ref):
    tiles = send_ref.shape[0]
    head_total = own_ref.shape[0]
    route = route_ref[0]
    of_tile = lax.broadcasted_iota(jnp.int32, route.shape, 0)
    codes = [pick_one(route, of_tile == tile) for tile in range(tiles)]
    for tile, code in enumerate(codes):

        @pl.when(code < head_total)
        def _():
            send_ref[tile] = own_ref[code]

        @pl.when(code >= head_total)
        def _():
            send_ref[tile] = got_ref[code - head_total]


def route_attend_kernel(
    counts_ref, route_ref, query_ref, own_ref, got_ref, more_ref, out_ref, scores, weights
):
    tiles = got_ref.shape[0]
    where = jnp.broadcast_to(route_ref[1, pl.ds(position(), 1), :], route_ref.shape[1:])
    of_head = lax.broadcasted_iota(jnp.int32, where.shape, 1)
    codes = [pick_one(where, of_head == head) for head in range(where.shape[1])]

    def far(head, which):
        code = codes[head]
        at = lax.rem(code, tiles)
        return jnp.where(code < tiles, got_ref[at, which], more_ref[at, which])

    attend(
        counts_ref,
        query_ref,
        lambda head: own_ref[head, 0],
        lambda head: own_ref[head, 1],
        lambda head: far(head, 0),
        lambda head: far(head, 1),
        out_ref,
        scores,
        weights,
    )


def attend_by_owner_kernel(
    counts_ref, query_ref, key_ref, value_ref, far_ref, out_ref, scores, weights
):
    inner = far_ref.shape[1] // 2
    attend(
        counts_ref,
        query_ref,
        lambda head: key_ref[:, head * DH : (head + 1) * DH],
        lambda head: value_ref[:, head * DH : (head + 1) * DH],
        lambda head: far_ref[head // inner, 2 * (head % inner)],
        lambda head: far_ref[head // inner, 2 * (head % inner) + 1],
        out_ref,
        scores,
        weights,
    )


def shards_by_route(query_states, key_states, value_states, tile_lists, tile_counts):
    rows, width = query_states.shape
    tiles = lax.axis_size(GROUP)
    head_total = width // DH
    dtype = key_states.dtype
    block = jax.ShapeDtypeStruct((tiles, 2, rows, DH), dtype)
    send, own, route, fail = pl.pallas_call(
        plan_kernel,
        out_shape=[
            block,
            jax.ShapeDtypeStruct((head_total, 2, rows, DH), dtype),
            jax.ShapeDtypeStruct((2, tiles, head_total), jnp.int32),
            jax.ShapeDtypeStruct((tiles, head_total), jnp.int32),
        ],
        in_specs=[VMEM, VMEM, ANY, ANY],
        out_specs=[VMEM] * 4,
        scratch_shapes=[pltpu.SemaphoreType.DMA((2 * head_total,))],
        compiler_params=PARAMS,
        name="plan",
    )(
        tile_lists.transpose(1, 2, 0),
        tile_counts.T,
        *(pltpu.with_memory_space_constraint(x, pltpu.HBM) for x in (key_states, value_states)),
    )
    got = lax.all_to_all(send, GROUP, split_axis=0, concat_axis=0, tiled=True)

    def routed(operands):
        query, _, _, _, counts, own, route, got = operands
        send = pl.pallas_call(
            forward_kernel,
            out_shape=block,
            in_specs=[VMEM] * 3,
            out_specs=VMEM,
            compiler_params=PARAMS,
            name="forward",
        )(route, own, got)
        more = lax.all_to_all(send, GROUP, split_axis=0, concat_axis=0, tiled=True)
        return pl.pallas_call(
            route_attend_kernel,
            out_shape=jax.ShapeDtypeStruct((rows, width), query.dtype),
            in_specs=[VMEM] * 6,
            out_specs=VMEM,
            scratch_shapes=attend_scratch(rows, width),
            compiler_params=PARAMS,
            name="attend",
        )(counts.T, route, query, own, got, more)

    def by_owner(operands):
        return shards_by_owner(*operands[:5])

    operands = (query_states, key_states, value_states, tile_lists, tile_counts, own, route, got)
    return lax.cond(fail[0, 0] > 0, by_owner, routed, operands)


def shards(query_states, key_states, value_states, tile_lists, tile_counts):
    rows = query_states.shape[0]
    head_total, tile_total, slots = tile_lists.shape
    owners = lax.axis_size(GROUP)
    one_tile = rows == TILE and tile_total == owners
    joins = tile_total * index_bits(tile_total) <= 24
    if one_tile and joins and slots == 2 and head_total % owners == 0:
        return shards_by_route(query_states, key_states, value_states, tile_lists, tile_counts)
    return shards_by_seq(query_states, key_states, value_states, tile_lists, tile_counts)


def solution(mesh):
    placed = (
        P(("clip", "seq", "help"), None),
        P(("clip", "seq", "help"), None),
        P(("clip", "seq", "help"), None),
        P("clip", None, None),
        P("clip", None),
    )
    return jax.shard_map(
        shards,
        mesh=mesh,
        in_specs=placed,
        out_specs=P(("clip", "seq", "help"), None),
        check_vma=False,
    )
```

```python
import math

import jax
import jax.numpy as jnp
from jax import lax
from jax.experimental import pallas as pl
from jax.experimental.pallas import tpu as pltpu
from jax.sharding import PartitionSpec as P

H = 16
DH = 128
TILE = 128
ROUND = 4


big_negative = -1e30


def pick_tiles(table, index):
    table_rows = table.shape[0]
    selector = (index[:, None] == jnp.arange(table_rows, dtype=jnp.int32)[None, :]).astype(
        jnp.bfloat16
    )
    picked = jnp.dot(selector, table.reshape(table_rows, -1), preferred_element_type=jnp.float32)
    return picked.astype(jnp.bfloat16).reshape((index.shape[0],) + table.shape[1:])


def attend_items(query_items, key_tiles, value_tiles, item_lists, item_counts):
    item_total, tile_rows, head_width = query_items.shape
    factor = head_width ** (-0.5)
    batches = item_total // ROUND
    joined = jnp.concatenate((key_tiles, value_tiles), axis=2)

    def one_batch(packed):
        queries, lists, counts = packed
        start_state = (
            jnp.full((ROUND, tile_rows, 1), big_negative, jnp.float32),
            jnp.zeros((ROUND, tile_rows, 1), jnp.float32),
            jnp.zeros((ROUND, tile_rows, head_width), jnp.float32),
        )

        def one_slot(slot_index, carried):
            running_max, running_sum, weighted = carried
            chosen = lax.dynamic_index_in_dim(lists, slot_index, axis=1, keepdims=False)
            both_blocks = pick_tiles(joined, chosen)
            key_block = both_blocks[:, :, :head_width]
            value_block = both_blocks[:, :, head_width:]
            scores = (
                jnp.einsum("qtd,qsd->qts", queries, key_block, preferred_element_type=jnp.float32)
                * factor
            )
            new_max = jnp.maximum(running_max, jnp.max(scores, axis=2, keepdims=True))
            shrink = jnp.exp(running_max - new_max)
            tile_weights = jnp.exp(scores - new_max)
            new_sum = running_sum * shrink + jnp.sum(tile_weights, axis=2, keepdims=True)
            new_weighted = weighted * shrink + jnp.einsum(
                "qts,qsd->qtd",
                tile_weights.astype(jnp.bfloat16),
                value_block,
                preferred_element_type=jnp.float32,
            )
            live = (slot_index < counts)[:, None, None]
            return (
                jnp.where(live, new_max, running_max),
                jnp.where(live, new_sum, running_sum),
                jnp.where(live, new_weighted, weighted),
            )

        final_state = lax.fori_loop(0, jnp.max(counts), one_slot, start_state)
        return (final_state[2] / final_state[1]).astype(jnp.bfloat16)

    finished = lax.map(
        one_batch,
        (
            query_items.reshape(batches, ROUND, tile_rows, head_width),
            item_lists.reshape(batches, ROUND, item_lists.shape[1]),
            item_counts.reshape(batches, ROUND),
        ),
    )
    return finished.reshape(item_total, tile_rows, head_width)


def shards_by_seq(query_states, key_states, value_states, tile_lists, tile_counts):
    groups = lax.axis_size("seq")
    helpers = lax.axis_size("help")
    device = lax.axis_index("seq")
    helper = lax.axis_index("help")
    row_count = query_states.shape[0]
    heads_here = H // groups
    head_cols = heads_here * DH
    tile_total = tile_lists.shape[1]
    per_block = row_count // TILE
    owned_total = groups * per_block

    def to_groups(states):
        return states.reshape(row_count, groups, head_cols)

    arrived = (
        lax.all_to_all(to_groups(query_states), "seq", split_axis=1, concat_axis=0, tiled=True),
        lax.all_to_all(to_groups(key_states), "seq", split_axis=1, concat_axis=0, tiled=True),
        lax.all_to_all(to_groups(value_states), "seq", split_axis=1, concat_axis=0, tiled=True),
    )
    arrived_query = arrived[0].reshape(groups, 1, row_count, head_cols)
    arrived_key = arrived[1].reshape(groups, 1, row_count, head_cols)
    arrived_value = arrived[2].reshape(groups, 1, row_count, head_cols)
    head_lists = lax.dynamic_slice_in_dim(tile_lists, device * heads_here, heads_here, 0)
    head_counts = lax.dynamic_slice_in_dim(tile_counts, device * heads_here, heads_here, 0)
    head_offset = (jnp.arange(heads_here, dtype=jnp.int32) * tile_total)[:, None, None]
    flat_lists = (head_lists + head_offset).reshape(heads_here * tile_total, head_lists.shape[2])
    flat_counts = head_counts.reshape(heads_here * tile_total)

    def head_tiles(whole):
        shaped = whole.reshape(tile_total, TILE, heads_here, DH).transpose(2, 0, 1, 3)
        return shaped.reshape(heads_here * tile_total, TILE, DH)

    key_whole, value_whole = (
        lax.all_gather(arrived_key, "help", axis=1, tiled=True),
        lax.all_gather(arrived_value, "help", axis=1, tiled=True),
    )
    key_tiles = head_tiles(key_whole)
    value_tiles = head_tiles(value_whole)
    own_tiles = arrived_query.reshape(owned_total, TILE, heads_here, DH).transpose(2, 0, 1, 3)
    own_tiles = own_tiles.reshape(heads_here * owned_total, TILE, DH)
    local_index = jnp.arange(owned_total, dtype=jnp.int32)
    global_tile = (
        local_index // per_block * helpers + helper
    ) * per_block + local_index % per_block
    item_index = (
        jnp.arange(heads_here, dtype=jnp.int32)[:, None] * tile_total + global_tile[None, :]
    )
    item_index = item_index.reshape(heads_here * owned_total)
    results = attend_items(
        own_tiles,
        key_tiles,
        value_tiles,
        jnp.take(flat_lists, item_index, axis=0),
        jnp.take(flat_counts, item_index, axis=0),
    )
    owned = results.reshape(heads_here, owned_total, TILE, DH)
    leaving = owned.transpose(1, 2, 0, 3)
    leaving = leaving.reshape(groups, row_count, head_cols)
    returned = lax.all_to_all(leaving, "seq", split_axis=0, concat_axis=2, tiled=True)
    return returned.reshape(row_count, H * DH)


GROUP = ("seq", "help")
ANY = pl.BlockSpec(memory_space=pl.ANY)
VMEM = pl.BlockSpec(memory_space=pltpu.VMEM)
PARAMS = pltpu.CompilerParams(vmem_limit_bytes=12 << 20)
STAGGER_NS = 7750


def position():
    return lax.axis_index("seq") * lax.axis_size("help") + lax.axis_index("help")


def pack_kernel(key_ref, value_ref, out_ref, sems):
    owners, parts = out_ref.shape[:2]
    reads = []
    for owner in range(owners):
        for part in range(parts):
            source = (key_ref, value_ref)[part % 2]
            head = owner * (parts // 2) + part // 2
            reads.append(
                pltpu.make_async_copy(
                    source.at[:, head * DH : (head + 1) * DH],
                    out_ref.at[owner, part],
                    sems.at[owner * parts + part],
                )
            )
            reads[-1].start()
    for read in reads:
        read.wait()


def index_bits(tiles):
    return (tiles - 1).bit_length()


def pick_kernel(lists_ref, held_ref, out_ref):
    tiles, parts = out_ref.shape[:2]
    heads = parts // 2
    bits = index_bits(tiles)
    first = position() * heads
    listed = lists_ref[:, 1, :]
    of_head = lax.broadcasted_iota(jnp.int32, listed.shape, 1)
    of_tile = lax.broadcasted_iota(jnp.int32, listed.shape, 0)
    placed = listed << (bits * of_tile)
    for head in range(heads):
        own = jnp.where(of_head == first + head, placed, 0).astype(jnp.float32)
        joined = jnp.sum(own).astype(jnp.int32)
        pair = slice(2 * head, 2 * head + 2)
        for tile in range(tiles):
            chosen = (joined >> (bits * tile)) & ((1 << bits) - 1)
            out_ref[tile, pair] = held_ref[chosen, pair]


def attend(counts_ref, query_ref, key, value, far_key, far_value, out_ref, scores, weights):
    width = query_ref.shape[1]
    factor = DH ** (-0.5) * math.log2(math.e)
    heads = range(width // DH)
    for head in heads:
        scores[head] = lax.dot_general(
            query_ref[:, head * DH : (head + 1) * DH],
            jnp.concatenate((key(head), far_key(head)), axis=0),
            (((1,), (1,)), ((), ())),
            preferred_element_type=jnp.float32,
        )
    counts = counts_ref[pl.ds(position(), 1), :]
    square = (counts.shape[1], counts.shape[1])
    own = lax.broadcasted_iota(jnp.int32, square, 0) == lax.broadcasted_iota(jnp.int32, square, 1)
    used = jnp.sum(jnp.where(own, counts, 0).astype(jnp.float32), axis=1, keepdims=True) > 1.5
    masks = jnp.where(jnp.broadcast_to(used, (square[0], TILE)), 0.0, big_negative)
    for head in heads:
        near = scores[head, :, :TILE]
        far = scores[head, :, TILE:] + masks[head : head + 1]
        top = jnp.max(jnp.maximum(near, far), axis=1, keepdims=True)
        weights[head, :, :TILE] = jnp.exp2((near - top) * factor).astype(weights.dtype)
        weights[head, :, TILE:] = jnp.exp2((far - top) * factor).astype(weights.dtype)
    for head in heads:
        values = jnp.concatenate((value(head), far_value(head)), axis=0)
        widened = jnp.concatenate((values, jnp.ones_like(values)), axis=1)
        product = jnp.dot(weights[head], widened, preferred_element_type=jnp.float32)
        out_ref[:, head * DH : (head + 1) * DH] = (product[:, :DH] / product[:, DH:]).astype(
            out_ref.dtype
        )


def attend_scratch(rows, width):
    shape = (width // DH, rows, 2 * TILE)
    return [pltpu.VMEM(shape, jnp.float32), pltpu.VMEM(shape, jnp.bfloat16)]


def shards_by_owner(query_states, key_states, value_states, tile_lists, tile_counts):
    rows, width = query_states.shape
    owners = lax.axis_size(GROUP)
    parts = 2 * width // DH // owners
    block = jax.ShapeDtypeStruct((owners, parts, rows, DH), key_states.dtype)
    packed = pl.pallas_call(
        pack_kernel,
        out_shape=block,
        in_specs=[ANY, ANY],
        out_specs=VMEM,
        scratch_shapes=[pltpu.SemaphoreType.DMA((owners * parts,))],
        compiler_params=PARAMS,
        name="pack",
    )(*(pltpu.with_memory_space_constraint(x, pltpu.HBM) for x in (key_states, value_states)))
    held = lax.all_to_all(packed, GROUP, split_axis=0, concat_axis=0, tiled=True)
    picked = pl.pallas_call(
        pick_kernel,
        out_shape=block,
        in_specs=[VMEM, VMEM],
        out_specs=VMEM,
        compiler_params=PARAMS,
        name="pick",
    )(tile_lists.transpose(1, 2, 0), held)
    far = lax.all_to_all(picked, GROUP, split_axis=0, concat_axis=0, tiled=True)
    return pl.pallas_call(
        attend_by_owner_kernel,
        out_shape=pltpu.HBM((rows, width), query_states.dtype),
        in_specs=[VMEM] * 5,
        out_specs=VMEM,
        scratch_shapes=attend_scratch(rows, width),
        compiler_params=PARAMS,
        name="attend",
    )(tile_counts.T, query_states, key_states, value_states, far)


def plan_kernel(
    lists_source,
    counts_source,
    key_ref,
    value_ref,
    send_ref,
    own_ref,
    route_ref,
    fail_ref,
    lists_ref,
    counts_ref,
    sems,
    table_sems,
):
    tiles, head_total = counts_ref.shape
    tables = [
        pltpu.make_async_copy(lists_source, lists_ref, table_sems.at[0]),
        pltpu.make_async_copy(counts_source, counts_ref, table_sems.at[1]),
    ]
    for table in tables:
        table.start()
    reads = []
    for head in range(head_total):
        for which, source in enumerate((key_ref, value_ref)):
            reads.append(
                pltpu.make_async_copy(
                    source.at[:, head * DH : (head + 1) * DH],
                    own_ref.at[head, which],
                    sems.at[2 * head + which],
                )
            )
            reads[-1].start()

    me = position()
    shape = (tiles, head_total)
    of_tile = lax.broadcasted_iota(jnp.int32, shape, 0)
    of_head = lax.broadcasted_iota(jnp.int32, shape, 1)
    for table in tables:
        table.wait()
    source = lists_ref[:, 1, :]
    wanted = counts_ref[...] > 1
    code = jnp.where(wanted, source, -1)
    rank = jnp.zeros(shape, jnp.int32)
    for head in range(head_total - 1):
        same = (code[:, head : head + 1] == source) & (of_head > head)
        rank = rank + same.astype(jnp.int32)
    first = wanted & (rank == 0)
    second = wanted & (rank == 1)
    further = wanted & (rank > 1)

    def along(block):
        total = jnp.sum(block.astype(jnp.float32), axis=1, keepdims=True)
        return jnp.broadcast_to(total.astype(jnp.int32), shape)

    def only(block):
        rows = jnp.sum(block.astype(jnp.float32), axis=1, keepdims=True)
        total = jnp.sum(rows, axis=0, keepdims=True)
        return jnp.broadcast_to(total.astype(jnp.int32), shape)

    def least(block):
        rows = jnp.min(block.astype(jnp.float32), axis=1, keepdims=True)
        lowest = jnp.min(rows, axis=0, keepdims=True)
        return jnp.broadcast_to(lowest.astype(jnp.int32), shape)

    bit = jnp.int32(1) << source
    mine = source == me
    none = 1 << 20
    state = (
        jnp.where(further, of_tile * head_total + of_head, none),
        first.astype(jnp.int32),
        along(jnp.where(first, bit, 0)),
        along(jnp.where(first, bit, 0)),
        along(jnp.where(second, bit, 0)),
        along(jnp.where(first & mine, of_head, 0)),
        along(jnp.where(second & mine, of_head, 0)),
        jnp.where(first, source, jnp.where(second, tiles + source, 0)),
        jnp.zeros(shape, jnp.int32),
    )

    def relay(_, state):
        key, direct, held1, movable, held2, send1, send2, where, fail = state
        here = key == least(key)
        to = only(jnp.where(here, of_tile, 0))
        head = only(jnp.where(here, of_head, 0))
        start = only(jnp.where(here, source, 0))
        held2_to = only(jnp.where((of_tile == to) & (of_head == 0), held2, 0))
        used1 = (held1 >> start) & 1
        fixed = 1 - ((movable >> start) & 1) * (1 - ((held2 >> start) & 1))
        free = ((held2_to >> of_tile) & 1) == 0
        free = free & (of_tile != start) & (of_tile != to) & ((used1 == 0) | (fixed == 0))
        best = least(jnp.where(free, of_tile + tiles * used1, none))
        good = best < none
        moved = good & (best >= tiles)
        via = jnp.where(moved, best - tiles, best)
        at_via = good & (of_tile == via)
        at_to = good & (of_tile == to)
        shifted = at_via & moved & (direct > 0) & (source == start)
        where = jnp.where(shifted, tiles + start, where)
        where = jnp.where(here & good, tiles + via, where)
        direct = jnp.where(shifted, 0, direct)
        send2 = jnp.where(at_via & moved & (start == me), send1, send2)
        send1 = jnp.where(at_via & (start == me), head, send1)
        send2 = jnp.where(at_to & (via == me), head_total + start, send2)
        start_bit = jnp.int32(1) << start
        held1 = jnp.where(at_via, held1 | start_bit, held1)
        movable = jnp.where(at_via, movable & ~start_bit, movable)
        held2 = jnp.where(at_via & moved, held2 | start_bit, held2)
        held2 = jnp.where(at_to, held2 | (jnp.int32(1) << jnp.where(good, via, 0)), held2)
        fail = jnp.where(good, fail, 1)
        key = jnp.where(here, none, key)
        return key, direct, held1, movable, held2, send1, send2, where, fail

    relays = jnp.sum(further.astype(jnp.float32)).astype(jnp.int32)
    state = lax.fori_loop(0, relays, relay, state)
    send1, send2, where, fail = state[5:]
    route_ref[0] = send2
    route_ref[1] = where
    fail_ref[...] = fail
    sent = [pick_one(send1, of_tile == tile) for tile in range(tiles)]
    if STAGGER_NS:
        @pl.when(lax.axis_index("clip") % 2 == 1)
        def _():
            pl.delay(STAGGER_NS)

    for read in reads:
        read.wait()
    writes = [
        pltpu.make_async_copy(own_ref.at[sent[tile]], send_ref.at[tile], sems.at[tile])
        for tile in range(tiles)
    ]
    for write in writes:
        write.start()
    for write in writes:
        write.wait()


def pick_one(block, at):
    return jnp.max(jnp.where(at, block, 0).astype(jnp.float32)).astype(jnp.int32)


def forward_kernel(route_ref, own_ref, got_ref, send_ref):
    tiles = send_ref.shape[0]
    head_total = own_ref.shape[0]
    route = route_ref[0]
    of_tile = lax.broadcasted_iota(jnp.int32, route.shape, 0)
    codes = [pick_one(route, of_tile == tile) for tile in range(tiles)]
    for tile, code in enumerate(codes):

        @pl.when(code < head_total)
        def _():
            send_ref[tile] = own_ref[code]

        @pl.when(code >= head_total)
        def _():
            send_ref[tile] = got_ref[code - head_total]


def route_attend_kernel(
    counts_ref, route_ref, query_ref, own_ref, got_ref, more_ref, out_ref, scores, weights
):
    tiles = got_ref.shape[0]
    where = jnp.broadcast_to(route_ref[1, pl.ds(position(), 1), :], route_ref.shape[1:])
    of_head = lax.broadcasted_iota(jnp.int32, where.shape, 1)
    codes = [pick_one(where, of_head == head) for head in range(where.shape[1])]

    def far(head, which):
        code = codes[head]
        at = lax.rem(code, tiles)
        return jnp.where(code < tiles, got_ref[at, which], more_ref[at, which])

    attend(
        counts_ref,
        query_ref,
        lambda head: own_ref[head, 0],
        lambda head: own_ref[head, 1],
        lambda head: far(head, 0),
        lambda head: far(head, 1),
        out_ref,
        scores,
        weights,
    )


def attend_by_owner_kernel(
    counts_ref, query_ref, key_ref, value_ref, far_ref, out_ref, scores, weights
):
    inner = far_ref.shape[1] // 2
    attend(
        counts_ref,
        query_ref,
        lambda head: key_ref[:, head * DH : (head + 1) * DH],
        lambda head: value_ref[:, head * DH : (head + 1) * DH],
        lambda head: far_ref[head // inner, 2 * (head % inner)],
        lambda head: far_ref[head // inner, 2 * (head % inner) + 1],
        out_ref,
        scores,
        weights,
    )


def shards_by_route(query_states, key_states, value_states, tile_lists, tile_counts):
    rows, width = query_states.shape
    tiles = lax.axis_size(GROUP)
    head_total = width // DH
    dtype = key_states.dtype
    block = jax.ShapeDtypeStruct((tiles, 2, rows, DH), dtype)
    send, own, route, fail = pl.pallas_call(
        plan_kernel,
        out_shape=[
            block,
            jax.ShapeDtypeStruct((head_total, 2, rows, DH), dtype),
            jax.ShapeDtypeStruct((2, tiles, head_total), jnp.int32),
            jax.ShapeDtypeStruct((tiles, head_total), jnp.int32),
        ],
        in_specs=[ANY] * 4,
        out_specs=[ANY] + [VMEM] * 3,
        scratch_shapes=[
            pltpu.VMEM((tiles, 2, head_total), jnp.int32),
            pltpu.VMEM((tiles, head_total), jnp.int32),
            pltpu.SemaphoreType.DMA((2 * head_total,)),
            pltpu.SemaphoreType.DMA((2,)),
        ],
        compiler_params=PARAMS,
        name="plan",
    )(
        *(
            pltpu.with_memory_space_constraint(x, pltpu.HBM)
            for x in (tile_lists.transpose(1, 2, 0), tile_counts.T, key_states, value_states)
        )
    )
    got = lax.all_to_all(send, GROUP, split_axis=0, concat_axis=0, tiled=True)

    def routed(operands):
        query, _, _, _, counts, own, route, got = operands
        send = pl.pallas_call(
            forward_kernel,
            out_shape=block,
            in_specs=[VMEM] * 3,
            out_specs=VMEM,
            compiler_params=PARAMS,
            name="forward",
        )(route, own, got)
        more = lax.all_to_all(send, GROUP, split_axis=0, concat_axis=0, tiled=True)
        return pl.pallas_call(
            route_attend_kernel,
            out_shape=pltpu.HBM((rows, width), query.dtype),
            in_specs=[VMEM] * 6,
            out_specs=VMEM,
            scratch_shapes=attend_scratch(rows, width),
            compiler_params=PARAMS,
            name="attend",
        )(counts.T, route, query, own, got, more)

    def by_owner(operands):
        return shards_by_owner(*operands[:5])

    operands = (query_states, key_states, value_states, tile_lists, tile_counts, own, route, got)
    return lax.cond(fail[0, 0] > 0, by_owner, routed, operands)


def shards(query_states, key_states, value_states, tile_lists, tile_counts):
    rows = query_states.shape[0]
    head_total, tile_total, slots = tile_lists.shape
    owners = lax.axis_size(GROUP)
    one_tile = rows == TILE and tile_total == owners
    joins = tile_total * index_bits(tile_total) <= 24
    if one_tile and joins and slots == 2 and head_total % owners == 0:
        return shards_by_route(query_states, key_states, value_states, tile_lists, tile_counts)
    return shards_by_seq(query_states, key_states, value_states, tile_lists, tile_counts)


def solution(mesh):
    placed = (
        P(("clip", "seq", "help"), None),
        P(("clip", "seq", "help"), None),
        P(("clip", "seq", "help"), None),
        P("clip", None, None),
        P("clip", None),
    )
    return jax.shard_map(
        shards,
        mesh=mesh,
        in_specs=placed,
        out_specs=P(("clip", "seq", "help"), None),
        check_vma=False,
    )
```

```python
import math

import jax
import jax.numpy as jnp
from jax import lax
from jax.experimental import pallas as pl
from jax.experimental.pallas import tpu as pltpu
from jax.sharding import PartitionSpec as P

H = 16
DH = 128
TILE = 128
ROUND = 4


big_negative = -1e30


def pick_tiles(table, index):
    table_rows = table.shape[0]
    selector = (index[:, None] == jnp.arange(table_rows, dtype=jnp.int32)[None, :]).astype(
        jnp.bfloat16
    )
    picked = jnp.dot(selector, table.reshape(table_rows, -1), preferred_element_type=jnp.float32)
    return picked.astype(jnp.bfloat16).reshape((index.shape[0],) + table.shape[1:])


def attend_items(query_items, key_tiles, value_tiles, item_lists, item_counts):
    item_total, tile_rows, head_width = query_items.shape
    factor = head_width ** (-0.5)
    batches = item_total // ROUND
    joined = jnp.concatenate((key_tiles, value_tiles), axis=2)

    def one_batch(packed):
        queries, lists, counts = packed
        start_state = (
            jnp.full((ROUND, tile_rows, 1), big_negative, jnp.float32),
            jnp.zeros((ROUND, tile_rows, 1), jnp.float32),
            jnp.zeros((ROUND, tile_rows, head_width), jnp.float32),
        )

        def one_slot(slot_index, carried):
            running_max, running_sum, weighted = carried
            chosen = lax.dynamic_index_in_dim(lists, slot_index, axis=1, keepdims=False)
            both_blocks = pick_tiles(joined, chosen)
            key_block = both_blocks[:, :, :head_width]
            value_block = both_blocks[:, :, head_width:]
            scores = (
                jnp.einsum("qtd,qsd->qts", queries, key_block, preferred_element_type=jnp.float32)
                * factor
            )
            new_max = jnp.maximum(running_max, jnp.max(scores, axis=2, keepdims=True))
            shrink = jnp.exp(running_max - new_max)
            tile_weights = jnp.exp(scores - new_max)
            new_sum = running_sum * shrink + jnp.sum(tile_weights, axis=2, keepdims=True)
            new_weighted = weighted * shrink + jnp.einsum(
                "qts,qsd->qtd",
                tile_weights.astype(jnp.bfloat16),
                value_block,
                preferred_element_type=jnp.float32,
            )
            live = (slot_index < counts)[:, None, None]
            return (
                jnp.where(live, new_max, running_max),
                jnp.where(live, new_sum, running_sum),
                jnp.where(live, new_weighted, weighted),
            )

        final_state = lax.fori_loop(0, jnp.max(counts), one_slot, start_state)
        return (final_state[2] / final_state[1]).astype(jnp.bfloat16)

    finished = lax.map(
        one_batch,
        (
            query_items.reshape(batches, ROUND, tile_rows, head_width),
            item_lists.reshape(batches, ROUND, item_lists.shape[1]),
            item_counts.reshape(batches, ROUND),
        ),
    )
    return finished.reshape(item_total, tile_rows, head_width)


def shards_by_seq(query_states, key_states, value_states, tile_lists, tile_counts):
    groups = lax.axis_size("seq")
    helpers = lax.axis_size("help")
    device = lax.axis_index("seq")
    helper = lax.axis_index("help")
    row_count = query_states.shape[0]
    heads_here = H // groups
    head_cols = heads_here * DH
    tile_total = tile_lists.shape[1]
    per_block = row_count // TILE
    owned_total = groups * per_block

    def to_groups(states):
        return states.reshape(row_count, groups, head_cols)

    arrived = (
        lax.all_to_all(to_groups(query_states), "seq", split_axis=1, concat_axis=0, tiled=True),
        lax.all_to_all(to_groups(key_states), "seq", split_axis=1, concat_axis=0, tiled=True),
        lax.all_to_all(to_groups(value_states), "seq", split_axis=1, concat_axis=0, tiled=True),
    )
    arrived_query = arrived[0].reshape(groups, 1, row_count, head_cols)
    arrived_key = arrived[1].reshape(groups, 1, row_count, head_cols)
    arrived_value = arrived[2].reshape(groups, 1, row_count, head_cols)
    head_lists = lax.dynamic_slice_in_dim(tile_lists, device * heads_here, heads_here, 0)
    head_counts = lax.dynamic_slice_in_dim(tile_counts, device * heads_here, heads_here, 0)
    head_offset = (jnp.arange(heads_here, dtype=jnp.int32) * tile_total)[:, None, None]
    flat_lists = (head_lists + head_offset).reshape(heads_here * tile_total, head_lists.shape[2])
    flat_counts = head_counts.reshape(heads_here * tile_total)

    def head_tiles(whole):
        shaped = whole.reshape(tile_total, TILE, heads_here, DH).transpose(2, 0, 1, 3)
        return shaped.reshape(heads_here * tile_total, TILE, DH)

    key_whole, value_whole = (
        lax.all_gather(arrived_key, "help", axis=1, tiled=True),
        lax.all_gather(arrived_value, "help", axis=1, tiled=True),
    )
    key_tiles = head_tiles(key_whole)
    value_tiles = head_tiles(value_whole)
    own_tiles = arrived_query.reshape(owned_total, TILE, heads_here, DH).transpose(2, 0, 1, 3)
    own_tiles = own_tiles.reshape(heads_here * owned_total, TILE, DH)
    local_index = jnp.arange(owned_total, dtype=jnp.int32)
    global_tile = (
        local_index // per_block * helpers + helper
    ) * per_block + local_index % per_block
    item_index = (
        jnp.arange(heads_here, dtype=jnp.int32)[:, None] * tile_total + global_tile[None, :]
    )
    item_index = item_index.reshape(heads_here * owned_total)
    results = attend_items(
        own_tiles,
        key_tiles,
        value_tiles,
        jnp.take(flat_lists, item_index, axis=0),
        jnp.take(flat_counts, item_index, axis=0),
    )
    owned = results.reshape(heads_here, owned_total, TILE, DH)
    leaving = owned.transpose(1, 2, 0, 3)
    leaving = leaving.reshape(groups, row_count, head_cols)
    returned = lax.all_to_all(leaving, "seq", split_axis=0, concat_axis=2, tiled=True)
    return returned.reshape(row_count, H * DH)


GROUP = ("seq", "help")
ANY = pl.BlockSpec(memory_space=pl.ANY)
VMEM = pl.BlockSpec(memory_space=pltpu.VMEM)
PARAMS = pltpu.CompilerParams(vmem_limit_bytes=12 << 20)
STAGGER_NS = 8000


def position():
    return lax.axis_index("seq") * lax.axis_size("help") + lax.axis_index("help")


def pack_kernel(key_ref, value_ref, out_ref, sems):
    owners, parts = out_ref.shape[:2]
    reads = []
    for owner in range(owners):
        for part in range(parts):
            source = (key_ref, value_ref)[part % 2]
            head = owner * (parts // 2) + part // 2
            reads.append(
                pltpu.make_async_copy(
                    source.at[:, head * DH : (head + 1) * DH],
                    out_ref.at[owner, part],
                    sems.at[owner * parts + part],
                )
            )
            reads[-1].start()
    for read in reads:
        read.wait()


def index_bits(tiles):
    return (tiles - 1).bit_length()


def pick_kernel(lists_ref, held_ref, out_ref):
    tiles, parts = out_ref.shape[:2]
    heads = parts // 2
    bits = index_bits(tiles)
    first = position() * heads
    listed = lists_ref[:, 1, :]
    of_head = lax.broadcasted_iota(jnp.int32, listed.shape, 1)
    of_tile = lax.broadcasted_iota(jnp.int32, listed.shape, 0)
    placed = listed << (bits * of_tile)
    for head in range(heads):
        own = jnp.where(of_head == first + head, placed, 0).astype(jnp.float32)
        joined = jnp.sum(own).astype(jnp.int32)
        pair = slice(2 * head, 2 * head + 2)
        for tile in range(tiles):
            chosen = (joined >> (bits * tile)) & ((1 << bits) - 1)
            out_ref[tile, pair] = held_ref[chosen, pair]


def attend(counts_ref, query_ref, key, value, far_key, far_value, out_ref, scores, weights):
    width = query_ref.shape[1]
    factor = DH ** (-0.5) * math.log2(math.e)
    heads = range(width // DH)
    for head in heads:
        scores[head] = lax.dot_general(
            query_ref[:, head * DH : (head + 1) * DH],
            jnp.concatenate((key(head), far_key(head)), axis=0),
            (((1,), (1,)), ((), ())),
            preferred_element_type=jnp.float32,
        )
    counts = counts_ref[pl.ds(position(), 1), :]
    square = (counts.shape[1], counts.shape[1])
    own = lax.broadcasted_iota(jnp.int32, square, 0) == lax.broadcasted_iota(jnp.int32, square, 1)
    used = jnp.sum(jnp.where(own, counts, 0).astype(jnp.float32), axis=1, keepdims=True) > 1.5
    masks = jnp.where(jnp.broadcast_to(used, (square[0], TILE)), 0.0, big_negative)
    for head in heads:
        near = scores[head, :, :TILE]
        far = scores[head, :, TILE:] + masks[head : head + 1]
        top = jnp.max(jnp.maximum(near, far), axis=1, keepdims=True)
        weights[head, :, :TILE] = jnp.exp2((near - top) * factor).astype(weights.dtype)
        weights[head, :, TILE:] = jnp.exp2((far - top) * factor).astype(weights.dtype)
    for head in heads:
        values = jnp.concatenate((value(head), far_value(head)), axis=0)
        widened = jnp.concatenate((values, jnp.ones_like(values)), axis=1)
        product = jnp.dot(weights[head], widened, preferred_element_type=jnp.float32)
        out_ref[:, head * DH : (head + 1) * DH] = (product[:, :DH] / product[:, DH:]).astype(
            out_ref.dtype
        )


def attend_scratch(rows, width):
    shape = (width // DH, rows, 2 * TILE)
    return [pltpu.VMEM(shape, jnp.float32), pltpu.VMEM(shape, jnp.bfloat16)]


def shards_by_owner(query_states, key_states, value_states, tile_lists, tile_counts):
    rows, width = query_states.shape
    owners = lax.axis_size(GROUP)
    parts = 2 * width // DH // owners
    block = jax.ShapeDtypeStruct((owners, parts, rows, DH), key_states.dtype)
    packed = pl.pallas_call(
        pack_kernel,
        out_shape=block,
        in_specs=[ANY, ANY],
        out_specs=VMEM,
        scratch_shapes=[pltpu.SemaphoreType.DMA((owners * parts,))],
        compiler_params=PARAMS,
        name="pack",
    )(*(pltpu.with_memory_space_constraint(x, pltpu.HBM) for x in (key_states, value_states)))
    held = lax.all_to_all(packed, GROUP, split_axis=0, concat_axis=0, tiled=True)
    picked = pl.pallas_call(
        pick_kernel,
        out_shape=block,
        in_specs=[VMEM, VMEM],
        out_specs=VMEM,
        compiler_params=PARAMS,
        name="pick",
    )(tile_lists.transpose(1, 2, 0), held)
    far = lax.all_to_all(picked, GROUP, split_axis=0, concat_axis=0, tiled=True)
    return pl.pallas_call(
        attend_by_owner_kernel,
        out_shape=pltpu.HBM((rows, width), query_states.dtype),
        in_specs=[VMEM] * 5,
        out_specs=VMEM,
        scratch_shapes=attend_scratch(rows, width),
        compiler_params=PARAMS,
        name="attend",
    )(tile_counts.T, query_states, key_states, value_states, far)


def plan_kernel(
    lists_source,
    counts_source,
    key_ref,
    value_ref,
    send_ref,
    own_ref,
    route_ref,
    fail_ref,
    lists_ref,
    counts_ref,
    sems,
    table_sems,
):
    tiles, head_total = counts_ref.shape
    tables = [
        pltpu.make_async_copy(lists_source, lists_ref, table_sems.at[0]),
        pltpu.make_async_copy(counts_source, counts_ref, table_sems.at[1]),
    ]
    for table in tables:
        table.start()
    reads = []
    for head in range(head_total):
        for which, source in enumerate((key_ref, value_ref)):
            reads.append(
                pltpu.make_async_copy(
                    source.at[:, head * DH : (head + 1) * DH],
                    own_ref.at[head, which],
                    sems.at[2 * head + which],
                )
            )
            reads[-1].start()

    me = position()
    shape = (tiles, head_total)
    of_tile = lax.broadcasted_iota(jnp.int32, shape, 0)
    of_head = lax.broadcasted_iota(jnp.int32, shape, 1)
    for table in tables:
        table.wait()
    source = lists_ref[:, 1, :]
    wanted = counts_ref[...] > 1
    code = jnp.where(wanted, source, -1)
    rank = jnp.zeros(shape, jnp.int32)
    for head in range(head_total - 1):
        same = (code[:, head : head + 1] == source) & (of_head > head)
        rank = rank + same.astype(jnp.int32)
    first = wanted & (rank == 0)
    second = wanted & (rank == 1)
    further = wanted & (rank > 1)

    def along(block):
        total = jnp.sum(block.astype(jnp.float32), axis=1, keepdims=True)
        return jnp.broadcast_to(total.astype(jnp.int32), shape)

    def least_of_all(block):
        rows = jnp.min(block.astype(jnp.float32), axis=1, keepdims=True)
        lowest = jnp.min(rows, axis=0, keepdims=True)
        return jnp.broadcast_to(lowest.astype(jnp.int32), shape)

    def over_tiles(reduce, block):
        return jnp.broadcast_to(reduce(block, axis=0, keepdims=True), shape)

    bit = jnp.int32(1) << source
    mine = source == me
    none = 1 << 20
    tile_bits, head_bits = index_bits(tiles), index_bits(head_total)
    key = (((of_tile << head_bits) | of_head) << tile_bits) | source
    taken = along(jnp.where(first, bit, 0))
    state = (
        jnp.where(further, key, none),
        first.astype(jnp.int32),
        taken,
        taken,
        along(jnp.where(second, bit, 0)),
        along(jnp.where(first & mine, of_head, 0)),
        along(jnp.where(second & mine, of_head, 0)),
        jnp.where(first, source, jnp.where(second, tiles + source, 0)),
        jnp.zeros(shape, jnp.int32),
    )

    def relay(_, state):
        key, direct, held1, movable, held2, send1, send2, where, fail = state
        lowest = least_of_all(key)
        here = key == lowest
        start = lowest & ((1 << tile_bits) - 1)
        head = (lowest >> tile_bits) & ((1 << head_bits) - 1)
        to = lowest >> (tile_bits + head_bits)
        held2_to = over_tiles(jnp.max, jnp.where(of_tile == to, held2, 0))
        used1 = (held1 >> start) & 1
        fixed = 1 - ((movable >> start) & 1) * (1 - ((held2 >> start) & 1))
        free = ((held2_to >> of_tile) & 1) == 0
        free = free & (of_tile != start) & (of_tile != to) & ((used1 == 0) | (fixed == 0))
        best = over_tiles(jnp.min, jnp.where(free, of_tile + tiles * used1, none))
        good = best < none
        moved = good & (best >= tiles)
        via = jnp.where(good, jnp.where(moved, best - tiles, best), 0)
        at_via = good & (of_tile == via)
        at_to = good & (of_tile == to)
        shifted = at_via & moved & (direct > 0) & (source == start)
        where = jnp.where(shifted, tiles + start, where)
        where = jnp.where(here & good, tiles + via, where)
        direct = jnp.where(shifted, 0, direct)
        send2 = jnp.where(at_via & moved & (start == me), send1, send2)
        send1 = jnp.where(at_via & (start == me), head, send1)
        send2 = jnp.where(at_to & (via == me), head_total + start, send2)
        start_bit = jnp.int32(1) << start
        held1 = jnp.where(at_via, held1 | start_bit, held1)
        movable = jnp.where(at_via, movable & ~start_bit, movable)
        held2 = jnp.where(at_via & moved, held2 | start_bit, held2)
        held2 = jnp.where(at_to, held2 | (jnp.int32(1) << via), held2)
        fail = jnp.where(good, fail, 1)
        key = jnp.where(here, none, key)
        return key, direct, held1, movable, held2, send1, send2, where, fail

    relays = jnp.sum(further.astype(jnp.float32)).astype(jnp.int32)
    state = lax.fori_loop(0, relays, relay, state)
    send1, send2, where, fail = state[5:]
    route_ref[0] = send2
    route_ref[1] = where
    fail_ref[...] = fail
    sent = [pick_one(send1, of_tile == tile) for tile in range(tiles)]
    if STAGGER_NS:
        @pl.when(lax.axis_index("clip") % 2 == 1)
        def _():
            pl.delay(STAGGER_NS)

    for read in reads:
        read.wait()
    writes = [
        pltpu.make_async_copy(own_ref.at[sent[tile]], send_ref.at[tile], sems.at[tile])
        for tile in range(tiles)
    ]
    for write in writes:
        write.start()
    for write in writes:
        write.wait()


def pick_one(block, at):
    return jnp.max(jnp.where(at, block, 0), axis=0, keepdims=True)[0, 0]


def forward_kernel(route_ref, own_ref, got_ref, send_ref):
    tiles = send_ref.shape[0]
    head_total = own_ref.shape[0]
    route = route_ref[0]
    of_tile = lax.broadcasted_iota(jnp.int32, route.shape, 0)
    codes = [pick_one(route, of_tile == tile) for tile in range(tiles)]
    for tile, code in enumerate(codes):

        @pl.when(code < head_total)
        def _():
            send_ref[tile] = own_ref[code]

        @pl.when(code >= head_total)
        def _():
            send_ref[tile] = got_ref[code - head_total]


def route_attend_kernel(
    counts_ref, route_ref, query_ref, own_ref, got_ref, more_ref, out_ref, scores, weights
):
    tiles = got_ref.shape[0]
    where = jnp.broadcast_to(route_ref[1, pl.ds(position(), 1), :], route_ref.shape[1:])
    codes = [where[0, head] for head in range(where.shape[1])]

    def far(head, which):
        code = codes[head]
        at = lax.rem(code, tiles)
        return jnp.where(code < tiles, got_ref[at, which], more_ref[at, which])

    attend(
        counts_ref,
        query_ref,
        lambda head: own_ref[head, 0],
        lambda head: own_ref[head, 1],
        lambda head: far(head, 0),
        lambda head: far(head, 1),
        out_ref,
        scores,
        weights,
    )


def attend_by_owner_kernel(
    counts_ref, query_ref, key_ref, value_ref, far_ref, out_ref, scores, weights
):
    inner = far_ref.shape[1] // 2
    attend(
        counts_ref,
        query_ref,
        lambda head: key_ref[:, head * DH : (head + 1) * DH],
        lambda head: value_ref[:, head * DH : (head + 1) * DH],
        lambda head: far_ref[head // inner, 2 * (head % inner)],
        lambda head: far_ref[head // inner, 2 * (head % inner) + 1],
        out_ref,
        scores,
        weights,
    )


def shards_by_route(query_states, key_states, value_states, tile_lists, tile_counts):
    rows, width = query_states.shape
    tiles = lax.axis_size(GROUP)
    head_total = width // DH
    dtype = key_states.dtype
    block = jax.ShapeDtypeStruct((tiles, 2, rows, DH), dtype)
    send, own, route, fail = pl.pallas_call(
        plan_kernel,
        out_shape=[
            block,
            jax.ShapeDtypeStruct((head_total, 2, rows, DH), dtype),
            jax.ShapeDtypeStruct((2, tiles, head_total), jnp.int32),
            jax.ShapeDtypeStruct((tiles, head_total), jnp.int32),
        ],
        in_specs=[ANY] * 4,
        out_specs=[ANY] + [VMEM] * 3,
        scratch_shapes=[
            pltpu.VMEM((tiles, 2, head_total), jnp.int32),
            pltpu.VMEM((tiles, head_total), jnp.int32),
            pltpu.SemaphoreType.DMA((2 * head_total,)),
            pltpu.SemaphoreType.DMA((2,)),
        ],
        compiler_params=PARAMS,
        name="plan",
    )(
        *(
            pltpu.with_memory_space_constraint(x, pltpu.HBM)
            for x in (tile_lists.transpose(1, 2, 0), tile_counts.T, key_states, value_states)
        )
    )
    got = lax.all_to_all(send, GROUP, split_axis=0, concat_axis=0, tiled=True)

    def routed(operands):
        query, _, _, _, counts, own, route, got = operands
        send = pl.pallas_call(
            forward_kernel,
            out_shape=block,
            in_specs=[VMEM] * 3,
            out_specs=VMEM,
            compiler_params=PARAMS,
            name="forward",
        )(route, own, got)
        more = lax.all_to_all(send, GROUP, split_axis=0, concat_axis=0, tiled=True)
        return pl.pallas_call(
            route_attend_kernel,
            out_shape=pltpu.HBM((rows, width), query.dtype),
            in_specs=[VMEM] * 6,
            out_specs=VMEM,
            scratch_shapes=attend_scratch(rows, width),
            compiler_params=PARAMS,
            name="attend",
        )(counts.T, route, query, own, got, more)

    def by_owner(operands):
        return shards_by_owner(*operands[:5])

    operands = (query_states, key_states, value_states, tile_lists, tile_counts, own, route, got)
    return lax.cond(fail[0, 0] > 0, by_owner, routed, operands)


def shards(query_states, key_states, value_states, tile_lists, tile_counts):
    rows = query_states.shape[0]
    head_total, tile_total, slots = tile_lists.shape
    owners = lax.axis_size(GROUP)
    one_tile = rows == TILE and tile_total == owners
    joins = tile_total * index_bits(tile_total) <= 24
    if one_tile and joins and slots == 2 and head_total % owners == 0:
        return shards_by_route(query_states, key_states, value_states, tile_lists, tile_counts)
    return shards_by_seq(query_states, key_states, value_states, tile_lists, tile_counts)


def solution(mesh):
    placed = (
        P(("clip", "seq", "help"), None),
        P(("clip", "seq", "help"), None),
        P(("clip", "seq", "help"), None),
        P("clip", None, None),
        P("clip", None),
    )
    return jax.shard_map(
        shards,
        mesh=mesh,
        in_specs=placed,
        out_specs=P(("clip", "seq", "help"), None),
        check_vma=False,
    )
```

```python
import math

import jax
import jax.numpy as jnp
from jax import lax
from jax.experimental import pallas as pl
from jax.experimental.pallas import tpu as pltpu
from jax.sharding import PartitionSpec as P

H = 16
DH = 128
TILE = 128
ROUND = 4


big_negative = -1e30


def pick_tiles(table, index):
    table_rows = table.shape[0]
    selector = (index[:, None] == jnp.arange(table_rows, dtype=jnp.int32)[None, :]).astype(
        jnp.bfloat16
    )
    picked = jnp.dot(selector, table.reshape(table_rows, -1), preferred_element_type=jnp.float32)
    return picked.astype(jnp.bfloat16).reshape((index.shape[0],) + table.shape[1:])


def attend_items(query_items, key_tiles, value_tiles, item_lists, item_counts):
    item_total, tile_rows, head_width = query_items.shape
    factor = head_width ** (-0.5)
    batches = item_total // ROUND
    joined = jnp.concatenate((key_tiles, value_tiles), axis=2)

    def one_batch(packed):
        queries, lists, counts = packed
        start_state = (
            jnp.full((ROUND, tile_rows, 1), big_negative, jnp.float32),
            jnp.zeros((ROUND, tile_rows, 1), jnp.float32),
            jnp.zeros((ROUND, tile_rows, head_width), jnp.float32),
        )

        def one_slot(slot_index, carried):
            running_max, running_sum, weighted = carried
            chosen = lax.dynamic_index_in_dim(lists, slot_index, axis=1, keepdims=False)
            both_blocks = pick_tiles(joined, chosen)
            key_block = both_blocks[:, :, :head_width]
            value_block = both_blocks[:, :, head_width:]
            scores = (
                jnp.einsum("qtd,qsd->qts", queries, key_block, preferred_element_type=jnp.float32)
                * factor
            )
            new_max = jnp.maximum(running_max, jnp.max(scores, axis=2, keepdims=True))
            shrink = jnp.exp(running_max - new_max)
            tile_weights = jnp.exp(scores - new_max)
            new_sum = running_sum * shrink + jnp.sum(tile_weights, axis=2, keepdims=True)
            new_weighted = weighted * shrink + jnp.einsum(
                "qts,qsd->qtd",
                tile_weights.astype(jnp.bfloat16),
                value_block,
                preferred_element_type=jnp.float32,
            )
            live = (slot_index < counts)[:, None, None]
            return (
                jnp.where(live, new_max, running_max),
                jnp.where(live, new_sum, running_sum),
                jnp.where(live, new_weighted, weighted),
            )

        final_state = lax.fori_loop(0, jnp.max(counts), one_slot, start_state)
        return (final_state[2] / final_state[1]).astype(jnp.bfloat16)

    finished = lax.map(
        one_batch,
        (
            query_items.reshape(batches, ROUND, tile_rows, head_width),
            item_lists.reshape(batches, ROUND, item_lists.shape[1]),
            item_counts.reshape(batches, ROUND),
        ),
    )
    return finished.reshape(item_total, tile_rows, head_width)


def shards_by_seq(query_states, key_states, value_states, tile_lists, tile_counts):
    groups = lax.axis_size("seq")
    helpers = lax.axis_size("help")
    device = lax.axis_index("seq")
    helper = lax.axis_index("help")
    row_count = query_states.shape[0]
    heads_here = H // groups
    head_cols = heads_here * DH
    tile_total = tile_lists.shape[1]
    per_block = row_count // TILE
    owned_total = groups * per_block

    def to_groups(states):
        return states.reshape(row_count, groups, head_cols)

    arrived = (
        lax.all_to_all(to_groups(query_states), "seq", split_axis=1, concat_axis=0, tiled=True),
        lax.all_to_all(to_groups(key_states), "seq", split_axis=1, concat_axis=0, tiled=True),
        lax.all_to_all(to_groups(value_states), "seq", split_axis=1, concat_axis=0, tiled=True),
    )
    arrived_query = arrived[0].reshape(groups, 1, row_count, head_cols)
    arrived_key = arrived[1].reshape(groups, 1, row_count, head_cols)
    arrived_value = arrived[2].reshape(groups, 1, row_count, head_cols)
    head_lists = lax.dynamic_slice_in_dim(tile_lists, device * heads_here, heads_here, 0)
    head_counts = lax.dynamic_slice_in_dim(tile_counts, device * heads_here, heads_here, 0)
    head_offset = (jnp.arange(heads_here, dtype=jnp.int32) * tile_total)[:, None, None]
    flat_lists = (head_lists + head_offset).reshape(heads_here * tile_total, head_lists.shape[2])
    flat_counts = head_counts.reshape(heads_here * tile_total)

    def head_tiles(whole):
        shaped = whole.reshape(tile_total, TILE, heads_here, DH).transpose(2, 0, 1, 3)
        return shaped.reshape(heads_here * tile_total, TILE, DH)

    key_whole, value_whole = (
        lax.all_gather(arrived_key, "help", axis=1, tiled=True),
        lax.all_gather(arrived_value, "help", axis=1, tiled=True),
    )
    key_tiles = head_tiles(key_whole)
    value_tiles = head_tiles(value_whole)
    own_tiles = arrived_query.reshape(owned_total, TILE, heads_here, DH).transpose(2, 0, 1, 3)
    own_tiles = own_tiles.reshape(heads_here * owned_total, TILE, DH)
    local_index = jnp.arange(owned_total, dtype=jnp.int32)
    global_tile = (
        local_index // per_block * helpers + helper
    ) * per_block + local_index % per_block
    item_index = (
        jnp.arange(heads_here, dtype=jnp.int32)[:, None] * tile_total + global_tile[None, :]
    )
    item_index = item_index.reshape(heads_here * owned_total)
    results = attend_items(
        own_tiles,
        key_tiles,
        value_tiles,
        jnp.take(flat_lists, item_index, axis=0),
        jnp.take(flat_counts, item_index, axis=0),
    )
    owned = results.reshape(heads_here, owned_total, TILE, DH)
    leaving = owned.transpose(1, 2, 0, 3)
    leaving = leaving.reshape(groups, row_count, head_cols)
    returned = lax.all_to_all(leaving, "seq", split_axis=0, concat_axis=2, tiled=True)
    return returned.reshape(row_count, H * DH)


GROUP = ("seq", "help")
ANY = pl.BlockSpec(memory_space=pl.ANY)
VMEM = pl.BlockSpec(memory_space=pltpu.VMEM)
PARAMS = pltpu.CompilerParams(vmem_limit_bytes=12 << 20)
STAGGER_NS = 7750


def position():
    return lax.axis_index("seq") * lax.axis_size("help") + lax.axis_index("help")


def pack_kernel(key_ref, value_ref, out_ref, sems):
    owners, parts = out_ref.shape[:2]
    reads = []
    for owner in range(owners):
        for part in range(parts):
            source = (key_ref, value_ref)[part % 2]
            head = owner * (parts // 2) + part // 2
            reads.append(
                pltpu.make_async_copy(
                    source.at[:, head * DH : (head + 1) * DH],
                    out_ref.at[owner, part],
                    sems.at[owner * parts + part],
                )
            )
            reads[-1].start()
    for read in reads:
        read.wait()


def index_bits(tiles):
    return (tiles - 1).bit_length()


def pick_kernel(lists_ref, held_ref, out_ref):
    tiles, parts = out_ref.shape[:2]
    heads = parts // 2
    bits = index_bits(tiles)
    first = position() * heads
    listed = lists_ref[:, 1, :]
    of_head = lax.broadcasted_iota(jnp.int32, listed.shape, 1)
    of_tile = lax.broadcasted_iota(jnp.int32, listed.shape, 0)
    placed = listed << (bits * of_tile)
    for head in range(heads):
        own = jnp.where(of_head == first + head, placed, 0).astype(jnp.float32)
        joined = jnp.sum(own).astype(jnp.int32)
        pair = slice(2 * head, 2 * head + 2)
        for tile in range(tiles):
            chosen = (joined >> (bits * tile)) & ((1 << bits) - 1)
            out_ref[tile, pair] = held_ref[chosen, pair]


def attend(counts_ref, query_ref, key, value, far_key, far_value, out_ref, scores, weights):
    width = query_ref.shape[1]
    factor = DH ** (-0.5) * math.log2(math.e)
    heads = width // DH
    counts = counts_ref[pl.ds(position(), 1), :]
    square = (counts.shape[1], counts.shape[1])
    own = lax.broadcasted_iota(jnp.int32, square, 0) == lax.broadcasted_iota(jnp.int32, square, 1)
    used = jnp.sum(jnp.where(own, counts, 0).astype(jnp.float32), axis=1, keepdims=True) > 1.5
    masks = jnp.where(jnp.broadcast_to(used, (square[0], TILE)), 0.0, big_negative)

    def score(head):
        scores[head] = lax.dot_general(
            query_ref[:, head * DH : (head + 1) * DH],
            jnp.concatenate((key(head), far_key(head)), axis=0),
            (((1,), (1,)), ((), ())),
            preferred_element_type=jnp.float32,
        )

    def weigh(head):
        near = scores[head, :, :TILE]
        far = scores[head, :, TILE:] + masks[head : head + 1]
        top = jnp.max(jnp.maximum(near, far), axis=1, keepdims=True)
        weights[head, :, :TILE] = jnp.exp2((near - top) * factor).astype(weights.dtype)
        weights[head, :, TILE:] = jnp.exp2((far - top) * factor).astype(weights.dtype)

    def gather(head):
        values = jnp.concatenate((value(head), far_value(head)), axis=0)
        widened = jnp.concatenate((values, jnp.ones_like(values)), axis=1)
        product = jnp.dot(weights[head], widened, preferred_element_type=jnp.float32)
        out_ref[:, head * DH : (head + 1) * DH] = (product[:, :DH] / product[:, DH:]).astype(
            out_ref.dtype
        )

    stages = ((0, score), (1, weigh), (2, gather))
    for step in range(heads + stages[-1][0]):
        for lag, stage in stages:
            if 0 <= step - lag < heads:
                stage(step - lag)


def attend_scratch(rows, width):
    shape = (width // DH, rows, 2 * TILE)
    return [pltpu.VMEM(shape, jnp.float32), pltpu.VMEM(shape, jnp.bfloat16)]


def shards_by_owner(query_states, key_states, value_states, tile_lists, tile_counts):
    rows, width = query_states.shape
    owners = lax.axis_size(GROUP)
    parts = 2 * width // DH // owners
    block = jax.ShapeDtypeStruct((owners, parts, rows, DH), key_states.dtype)
    packed = pl.pallas_call(
        pack_kernel,
        out_shape=block,
        in_specs=[ANY, ANY],
        out_specs=VMEM,
        scratch_shapes=[pltpu.SemaphoreType.DMA((owners * parts,))],
        compiler_params=PARAMS,
        name="pack",
    )(*(pltpu.with_memory_space_constraint(x, pltpu.HBM) for x in (key_states, value_states)))
    held = lax.all_to_all(packed, GROUP, split_axis=0, concat_axis=0, tiled=True)
    picked = pl.pallas_call(
        pick_kernel,
        out_shape=block,
        in_specs=[VMEM, VMEM],
        out_specs=VMEM,
        compiler_params=PARAMS,
        name="pick",
    )(tile_lists.transpose(1, 2, 0), held)
    far = lax.all_to_all(picked, GROUP, split_axis=0, concat_axis=0, tiled=True)
    return pl.pallas_call(
        attend_by_owner_kernel,
        out_shape=pltpu.HBM((rows, width), query_states.dtype),
        in_specs=[VMEM] * 5,
        out_specs=VMEM,
        scratch_shapes=attend_scratch(rows, width),
        compiler_params=PARAMS,
        name="attend",
    )(tile_counts.T, query_states, key_states, value_states, far)


def plan_kernel(
    lists_source,
    counts_source,
    key_ref,
    value_ref,
    send_ref,
    own_ref,
    route_ref,
    fail_ref,
    lists_ref,
    counts_ref,
    sems,
    table_sems,
):
    tiles, head_total = counts_ref.shape
    tables = [
        pltpu.make_async_copy(lists_source, lists_ref, table_sems.at[0]),
        pltpu.make_async_copy(counts_source, counts_ref, table_sems.at[1]),
    ]
    for table in tables:
        table.start()
    for head in range(head_total):
        for which, source in enumerate((key_ref, value_ref)):
            pltpu.make_async_copy(
                source.at[:, head * DH : (head + 1) * DH], own_ref.at[head, which], sems.at[0]
            ).start()
    all_read = pltpu.make_async_copy(own_ref, own_ref, sems.at[0])

    me = position()
    shape = (tiles, head_total)
    of_tile = lax.broadcasted_iota(jnp.int32, shape, 0)
    of_head = lax.broadcasted_iota(jnp.int32, shape, 1)
    for table in tables:
        table.wait()
    source = lists_ref[:, 1, :]
    wanted = counts_ref[...] > 1
    code = jnp.where(wanted, source, -1)
    rank = jnp.zeros(shape, jnp.int32)
    for head in range(head_total - 1):
        same = (code[:, head : head + 1] == source) & (of_head > head)
        rank = rank + same.astype(jnp.int32)
    first = wanted & (rank == 0)
    second = wanted & (rank == 1)
    further = wanted & (rank > 1)

    def along(block):
        total = jnp.sum(block.astype(jnp.float32), axis=1, keepdims=True)
        return jnp.broadcast_to(total.astype(jnp.int32), shape)

    def least_of_all(block):
        rows = jnp.min(block.astype(jnp.float32), axis=1, keepdims=True)
        lowest = jnp.min(rows, axis=0, keepdims=True)
        return jnp.broadcast_to(lowest.astype(jnp.int32), shape)

    def over_tiles(reduce, block):
        return jnp.broadcast_to(reduce(block, axis=0, keepdims=True), shape)

    bit = jnp.int32(1) << source
    mine = source == me
    none = 1 << 20
    tile_bits, head_bits = index_bits(tiles), index_bits(head_total)
    key = (((of_tile << head_bits) | of_head) << tile_bits) | source
    taken = along(jnp.where(first, bit, 0))
    state = (
        jnp.where(further, key, none),
        first.astype(jnp.int32),
        taken,
        taken,
        along(jnp.where(second, bit, 0)),
        along(jnp.where(first & mine, of_head, 0)),
        along(jnp.where(second & mine, of_head, 0)),
        jnp.where(first, source, jnp.where(second, tiles + source, 0)),
        jnp.zeros(shape, jnp.int32),
    )

    def relay(_, state):
        key, direct, held1, movable, held2, send1, send2, where, fail = state
        lowest = least_of_all(key)
        here = key == lowest
        start = lowest & ((1 << tile_bits) - 1)
        head = (lowest >> tile_bits) & ((1 << head_bits) - 1)
        to = lowest >> (tile_bits + head_bits)
        held2_to = over_tiles(jnp.max, jnp.where(of_tile == to, held2, 0))
        used1 = (held1 >> start) & 1
        fixed = 1 - ((movable >> start) & 1) * (1 - ((held2 >> start) & 1))
        free = ((held2_to >> of_tile) & 1) == 0
        free = free & (of_tile != start) & (of_tile != to) & ((used1 == 0) | (fixed == 0))
        best = over_tiles(jnp.min, jnp.where(free, of_tile + tiles * used1, none))
        good = best < none
        moved = good & (best >= tiles)
        via = jnp.where(good, jnp.where(moved, best - tiles, best), 0)
        at_via = good & (of_tile == via)
        at_to = good & (of_tile == to)
        shifted = at_via & moved & (direct > 0) & (source == start)
        where = jnp.where(shifted, tiles + start, where)
        where = jnp.where(here & good, tiles + via, where)
        direct = jnp.where(shifted, 0, direct)
        send2 = jnp.where(at_via & moved & (start == me), send1, send2)
        send1 = jnp.where(at_via & (start == me), head, send1)
        send2 = jnp.where(at_to & (via == me), head_total + start, send2)
        start_bit = jnp.int32(1) << start
        held1 = jnp.where(at_via, held1 | start_bit, held1)
        movable = jnp.where(at_via, movable & ~start_bit, movable)
        held2 = jnp.where(at_via & moved, held2 | start_bit, held2)
        held2 = jnp.where(at_to, held2 | (jnp.int32(1) << via), held2)
        fail = jnp.where(good, fail, 1)
        key = jnp.where(here, none, key)
        return key, direct, held1, movable, held2, send1, send2, where, fail

    relays = jnp.sum(further.astype(jnp.float32)).astype(jnp.int32)
    state = lax.fori_loop(0, relays, relay, state)
    send1, send2, where, fail = state[5:]
    route_ref[0] = send2
    route_ref[1] = where
    fail_ref[...] = fail
    sent = [pick_one(send1, of_tile == tile) for tile in range(tiles)]
    if STAGGER_NS:
        @pl.when(lax.axis_index("clip") % 2 == 1)
        def _():
            pl.delay(STAGGER_NS)

    all_read.wait()
    writes = [
        pltpu.make_async_copy(own_ref.at[sent[tile]], send_ref.at[tile], sems.at[1])
        for tile in range(tiles)
    ]
    for write in writes:
        write.start()
    pltpu.make_async_copy(own_ref.at[pl.ds(0, tiles)], send_ref, sems.at[1]).wait()


def pick_one(block, at):
    return jnp.max(jnp.where(at, block, 0), axis=0, keepdims=True)[0, 0]


def forward_kernel(route_ref, own_ref, got_ref, send_ref):
    tiles = send_ref.shape[0]
    head_total = own_ref.shape[0]
    route = route_ref[0]
    of_tile = lax.broadcasted_iota(jnp.int32, route.shape, 0)
    codes = [pick_one(route, of_tile == tile) for tile in range(tiles)]
    for tile, code in enumerate(codes):

        @pl.when(code < head_total)
        def _():
            send_ref[tile] = own_ref[code]

        @pl.when(code >= head_total)
        def _():
            send_ref[tile] = got_ref[code - head_total]


def route_attend_kernel(
    counts_ref, route_ref, query_ref, own_ref, got_ref, more_ref, out_ref, scores, weights
):
    tiles = got_ref.shape[0]
    where = jnp.broadcast_to(route_ref[1, pl.ds(position(), 1), :], route_ref.shape[1:])
    codes = [where[0, head] for head in range(where.shape[1])]

    def far(head, which):
        code = codes[head]
        at = lax.rem(code, tiles)
        return jnp.where(code < tiles, got_ref[at, which], more_ref[at, which])

    attend(
        counts_ref,
        query_ref,
        lambda head: own_ref[head, 0],
        lambda head: own_ref[head, 1],
        lambda head: far(head, 0),
        lambda head: far(head, 1),
        out_ref,
        scores,
        weights,
    )


def attend_by_owner_kernel(
    counts_ref, query_ref, key_ref, value_ref, far_ref, out_ref, scores, weights
):
    inner = far_ref.shape[1] // 2
    attend(
        counts_ref,
        query_ref,
        lambda head: key_ref[:, head * DH : (head + 1) * DH],
        lambda head: value_ref[:, head * DH : (head + 1) * DH],
        lambda head: far_ref[head // inner, 2 * (head % inner)],
        lambda head: far_ref[head // inner, 2 * (head % inner) + 1],
        out_ref,
        scores,
        weights,
    )


def shards_by_route(query_states, key_states, value_states, tile_lists, tile_counts):
    rows, width = query_states.shape
    tiles = lax.axis_size(GROUP)
    head_total = width // DH
    dtype = key_states.dtype
    block = jax.ShapeDtypeStruct((tiles, 2, rows, DH), dtype)
    send, own, route, fail = pl.pallas_call(
        plan_kernel,
        out_shape=[
            block,
            jax.ShapeDtypeStruct((head_total, 2, rows, DH), dtype),
            jax.ShapeDtypeStruct((2, tiles, head_total), jnp.int32),
            jax.ShapeDtypeStruct((tiles, head_total), jnp.int32),
        ],
        in_specs=[ANY] * 4,
        out_specs=[ANY] + [VMEM] * 3,
        scratch_shapes=[
            pltpu.VMEM((tiles, 2, head_total), jnp.int32),
            pltpu.VMEM((tiles, head_total), jnp.int32),
            pltpu.SemaphoreType.DMA((2,)),
            pltpu.SemaphoreType.DMA((2,)),
        ],
        compiler_params=PARAMS,
        name="plan",
    )(
        *(
            pltpu.with_memory_space_constraint(x, pltpu.HBM)
            for x in (tile_lists.transpose(1, 2, 0), tile_counts.T, key_states, value_states)
        )
    )
    got = lax.all_to_all(send, GROUP, split_axis=0, concat_axis=0, tiled=True)

    def routed(operands):
        query, _, _, _, counts, own, route, got = operands
        send = pl.pallas_call(
            forward_kernel,
            out_shape=block,
            in_specs=[VMEM] * 3,
            out_specs=VMEM,
            compiler_params=PARAMS,
            name="forward",
        )(route, own, got)
        more = lax.all_to_all(send, GROUP, split_axis=0, concat_axis=0, tiled=True)
        return pl.pallas_call(
            route_attend_kernel,
            out_shape=pltpu.HBM((rows, width), query.dtype),
            in_specs=[VMEM] * 6,
            out_specs=VMEM,
            scratch_shapes=attend_scratch(rows, width),
            compiler_params=PARAMS,
            name="attend",
        )(counts.T, route, query, own, got, more)

    def by_owner(operands):
        return shards_by_owner(*operands[:5])

    operands = (query_states, key_states, value_states, tile_lists, tile_counts, own, route, got)
    return lax.cond(fail[0, 0] > 0, by_owner, routed, operands)


def shards(query_states, key_states, value_states, tile_lists, tile_counts):
    rows = query_states.shape[0]
    head_total, tile_total, slots = tile_lists.shape
    owners = lax.axis_size(GROUP)
    one_tile = rows == TILE and tile_total == owners
    joins = tile_total * index_bits(tile_total) <= 24
    if one_tile and joins and slots == 2 and head_total % owners == 0:
        return shards_by_route(query_states, key_states, value_states, tile_lists, tile_counts)
    return shards_by_seq(query_states, key_states, value_states, tile_lists, tile_counts)


def solution(mesh):
    placed = (
        P(("clip", "seq", "help"), None),
        P(("clip", "seq", "help"), None),
        P(("clip", "seq", "help"), None),
        P("clip", None, None),
        P("clip", None),
    )
    return jax.shard_map(
        shards,
        mesh=mesh,
        in_specs=placed,
        out_specs=P(("clip", "seq", "help"), None),
        check_vma=False,
    )
```

```python
import math

import jax
import jax.numpy as jnp
from jax import lax
from jax.experimental import pallas as pl
from jax.experimental.pallas import tpu as pltpu
from jax.sharding import PartitionSpec as P

H = 16
DH = 128
TILE = 128
ROUND = 4


big_negative = -1e30


def pick_tiles(table, index):
    table_rows = table.shape[0]
    selector = (index[:, None] == jnp.arange(table_rows, dtype=jnp.int32)[None, :]).astype(
        jnp.bfloat16
    )
    picked = jnp.dot(selector, table.reshape(table_rows, -1), preferred_element_type=jnp.float32)
    return picked.astype(jnp.bfloat16).reshape((index.shape[0],) + table.shape[1:])


def attend_items(query_items, key_tiles, value_tiles, item_lists, item_counts):
    item_total, tile_rows, head_width = query_items.shape
    factor = head_width ** (-0.5)
    batches = item_total // ROUND
    joined = jnp.concatenate((key_tiles, value_tiles), axis=2)

    def one_batch(packed):
        queries, lists, counts = packed
        start_state = (
            jnp.full((ROUND, tile_rows, 1), big_negative, jnp.float32),
            jnp.zeros((ROUND, tile_rows, 1), jnp.float32),
            jnp.zeros((ROUND, tile_rows, head_width), jnp.float32),
        )

        def one_slot(slot_index, carried):
            running_max, running_sum, weighted = carried
            chosen = lax.dynamic_index_in_dim(lists, slot_index, axis=1, keepdims=False)
            both_blocks = pick_tiles(joined, chosen)
            key_block = both_blocks[:, :, :head_width]
            value_block = both_blocks[:, :, head_width:]
            scores = (
                jnp.einsum("qtd,qsd->qts", queries, key_block, preferred_element_type=jnp.float32)
                * factor
            )
            new_max = jnp.maximum(running_max, jnp.max(scores, axis=2, keepdims=True))
            shrink = jnp.exp(running_max - new_max)
            tile_weights = jnp.exp(scores - new_max)
            new_sum = running_sum * shrink + jnp.sum(tile_weights, axis=2, keepdims=True)
            new_weighted = weighted * shrink + jnp.einsum(
                "qts,qsd->qtd",
                tile_weights.astype(jnp.bfloat16),
                value_block,
                preferred_element_type=jnp.float32,
            )
            live = (slot_index < counts)[:, None, None]
            return (
                jnp.where(live, new_max, running_max),
                jnp.where(live, new_sum, running_sum),
                jnp.where(live, new_weighted, weighted),
            )

        final_state = lax.fori_loop(0, jnp.max(counts), one_slot, start_state)
        return (final_state[2] / final_state[1]).astype(jnp.bfloat16)

    finished = lax.map(
        one_batch,
        (
            query_items.reshape(batches, ROUND, tile_rows, head_width),
            item_lists.reshape(batches, ROUND, item_lists.shape[1]),
            item_counts.reshape(batches, ROUND),
        ),
    )
    return finished.reshape(item_total, tile_rows, head_width)


def shards_by_seq(query_states, key_states, value_states, tile_lists, tile_counts):
    groups = lax.axis_size("seq")
    helpers = lax.axis_size("help")
    device = lax.axis_index("seq")
    helper = lax.axis_index("help")
    row_count = query_states.shape[0]
    heads_here = H // groups
    head_cols = heads_here * DH
    tile_total = tile_lists.shape[1]
    per_block = row_count // TILE
    owned_total = groups * per_block

    def to_groups(states):
        return states.reshape(row_count, groups, head_cols)

    arrived = (
        lax.all_to_all(to_groups(query_states), "seq", split_axis=1, concat_axis=0, tiled=True),
        lax.all_to_all(to_groups(key_states), "seq", split_axis=1, concat_axis=0, tiled=True),
        lax.all_to_all(to_groups(value_states), "seq", split_axis=1, concat_axis=0, tiled=True),
    )
    arrived_query = arrived[0].reshape(groups, 1, row_count, head_cols)
    arrived_key = arrived[1].reshape(groups, 1, row_count, head_cols)
    arrived_value = arrived[2].reshape(groups, 1, row_count, head_cols)
    head_lists = lax.dynamic_slice_in_dim(tile_lists, device * heads_here, heads_here, 0)
    head_counts = lax.dynamic_slice_in_dim(tile_counts, device * heads_here, heads_here, 0)
    head_offset = (jnp.arange(heads_here, dtype=jnp.int32) * tile_total)[:, None, None]
    flat_lists = (head_lists + head_offset).reshape(heads_here * tile_total, head_lists.shape[2])
    flat_counts = head_counts.reshape(heads_here * tile_total)

    def head_tiles(whole):
        shaped = whole.reshape(tile_total, TILE, heads_here, DH).transpose(2, 0, 1, 3)
        return shaped.reshape(heads_here * tile_total, TILE, DH)

    key_whole, value_whole = (
        lax.all_gather(arrived_key, "help", axis=1, tiled=True),
        lax.all_gather(arrived_value, "help", axis=1, tiled=True),
    )
    key_tiles = head_tiles(key_whole)
    value_tiles = head_tiles(value_whole)
    own_tiles = arrived_query.reshape(owned_total, TILE, heads_here, DH).transpose(2, 0, 1, 3)
    own_tiles = own_tiles.reshape(heads_here * owned_total, TILE, DH)
    local_index = jnp.arange(owned_total, dtype=jnp.int32)
    global_tile = (
        local_index // per_block * helpers + helper
    ) * per_block + local_index % per_block
    item_index = (
        jnp.arange(heads_here, dtype=jnp.int32)[:, None] * tile_total + global_tile[None, :]
    )
    item_index = item_index.reshape(heads_here * owned_total)
    results = attend_items(
        own_tiles,
        key_tiles,
        value_tiles,
        jnp.take(flat_lists, item_index, axis=0),
        jnp.take(flat_counts, item_index, axis=0),
    )
    owned = results.reshape(heads_here, owned_total, TILE, DH)
    leaving = owned.transpose(1, 2, 0, 3)
    leaving = leaving.reshape(groups, row_count, head_cols)
    returned = lax.all_to_all(leaving, "seq", split_axis=0, concat_axis=2, tiled=True)
    return returned.reshape(row_count, H * DH)


GROUP = ("seq", "help")
ANY = pl.BlockSpec(memory_space=pl.ANY)
VMEM = pl.BlockSpec(memory_space=pltpu.VMEM)
PARAMS = pltpu.CompilerParams(vmem_limit_bytes=12 << 20)
STAGGER_NS = 8000


def position():
    return lax.axis_index("seq") * lax.axis_size("help") + lax.axis_index("help")


def pack_kernel(key_ref, value_ref, out_ref, sems):
    owners, parts = out_ref.shape[:2]
    reads = []
    for owner in range(owners):
        for part in range(parts):
            source = (key_ref, value_ref)[part % 2]
            head = owner * (parts // 2) + part // 2
            reads.append(
                pltpu.make_async_copy(
                    source.at[:, head * DH : (head + 1) * DH],
                    out_ref.at[owner, part],
                    sems.at[owner * parts + part],
                )
            )
            reads[-1].start()
    for read in reads:
        read.wait()


def index_bits(tiles):
    return (tiles - 1).bit_length()


def pick_kernel(lists_ref, held_ref, out_ref):
    tiles, parts = out_ref.shape[:2]
    heads = parts // 2
    bits = index_bits(tiles)
    first = position() * heads
    listed = lists_ref[:, 1, :]
    of_head = lax.broadcasted_iota(jnp.int32, listed.shape, 1)
    of_tile = lax.broadcasted_iota(jnp.int32, listed.shape, 0)
    placed = listed << (bits * of_tile)
    for head in range(heads):
        own = jnp.where(of_head == first + head, placed, 0).astype(jnp.float32)
        joined = jnp.sum(own).astype(jnp.int32)
        pair = slice(2 * head, 2 * head + 2)
        for tile in range(tiles):
            chosen = (joined >> (bits * tile)) & ((1 << bits) - 1)
            out_ref[tile, pair] = held_ref[chosen, pair]


def attend(counts_ref, query_ref, key, value, far_key, far_value, out_ref, scores, weights):
    width = query_ref.shape[1]
    factor = DH ** (-0.5) * math.log2(math.e)
    heads = width // DH
    counts = counts_ref[pl.ds(position(), 1), :]
    square = (counts.shape[1], counts.shape[1])
    own = lax.broadcasted_iota(jnp.int32, square, 0) == lax.broadcasted_iota(jnp.int32, square, 1)
    used = jnp.sum(jnp.where(own, counts, 0).astype(jnp.float32), axis=1, keepdims=True) > 1.5
    masks = jnp.where(jnp.broadcast_to(used, (square[0], TILE)), 0.0, big_negative)

    def score(head):
        scores[head] = lax.dot_general(
            query_ref[:, head * DH : (head + 1) * DH],
            jnp.concatenate((key(head), far_key(head)), axis=0),
            (((1,), (1,)), ((), ())),
            preferred_element_type=jnp.float32,
        )

    def weigh(head):
        near = scores[head, :, :TILE]
        far = scores[head, :, TILE:] + masks[head : head + 1]
        top = jnp.max(jnp.maximum(near, far), axis=1, keepdims=True)
        weights[head, :, :TILE] = jnp.exp2((near - top) * factor).astype(weights.dtype)
        weights[head, :, TILE:] = jnp.exp2((far - top) * factor).astype(weights.dtype)

    def gather(head):
        values = jnp.concatenate((value(head), far_value(head)), axis=0)
        widened = jnp.concatenate((values, jnp.ones_like(values)), axis=1)
        product = jnp.dot(weights[head], widened, preferred_element_type=jnp.float32)
        out_ref[:, head * DH : (head + 1) * DH] = (product[:, :DH] / product[:, DH:]).astype(
            out_ref.dtype
        )

    stages = ((0, score), (1, weigh), (2, gather))
    for step in range(heads + stages[-1][0]):
        for lag, stage in stages:
            if 0 <= step - lag < heads:
                stage(step - lag)


def attend_scratch(rows, width):
    shape = (width // DH, rows, 2 * TILE)
    return [pltpu.VMEM(shape, jnp.float32), pltpu.VMEM(shape, jnp.bfloat16)]


def shards_by_owner(query_states, key_states, value_states, tile_lists, tile_counts):
    rows, width = query_states.shape
    owners = lax.axis_size(GROUP)
    parts = 2 * width // DH // owners
    block = jax.ShapeDtypeStruct((owners, parts, rows, DH), key_states.dtype)
    packed = pl.pallas_call(
        pack_kernel,
        out_shape=block,
        in_specs=[ANY, ANY],
        out_specs=VMEM,
        scratch_shapes=[pltpu.SemaphoreType.DMA((owners * parts,))],
        compiler_params=PARAMS,
        name="pack",
    )(*(pltpu.with_memory_space_constraint(x, pltpu.HBM) for x in (key_states, value_states)))
    held = lax.all_to_all(packed, GROUP, split_axis=0, concat_axis=0, tiled=True)
    picked = pl.pallas_call(
        pick_kernel,
        out_shape=block,
        in_specs=[VMEM, VMEM],
        out_specs=VMEM,
        compiler_params=PARAMS,
        name="pick",
    )(tile_lists.transpose(1, 2, 0), held)
    far = lax.all_to_all(picked, GROUP, split_axis=0, concat_axis=0, tiled=True)
    return pl.pallas_call(
        attend_by_owner_kernel,
        out_shape=pltpu.HBM((rows, width), query_states.dtype),
        in_specs=[VMEM] * 5,
        out_specs=VMEM,
        scratch_shapes=attend_scratch(rows, width),
        compiler_params=PARAMS,
        name="attend",
    )(tile_counts.T, query_states, key_states, value_states, far)


def plan_kernel(
    lists_source,
    counts_source,
    key_ref,
    value_ref,
    send_ref,
    own_ref,
    route_ref,
    fail_ref,
    lists_ref,
    counts_ref,
    sems,
    table_sems,
):
    tiles, head_total = counts_ref.shape
    tables = [
        pltpu.make_async_copy(lists_source, lists_ref, table_sems.at[0]),
        pltpu.make_async_copy(counts_source, counts_ref, table_sems.at[1]),
    ]
    for table in tables:
        table.start()
    for head in range(head_total):
        for which, source in enumerate((key_ref, value_ref)):
            pltpu.make_async_copy(
                source.at[:, head * DH : (head + 1) * DH], own_ref.at[head, which], sems.at[0]
            ).start()
    all_read = pltpu.make_async_copy(own_ref, own_ref, sems.at[0])

    me = position()
    shape = (tiles, head_total)
    of_tile = lax.broadcasted_iota(jnp.int32, shape, 0)
    of_head = lax.broadcasted_iota(jnp.int32, shape, 1)
    for table in tables:
        table.wait()
    source = lists_ref[:, 1, :]
    wanted = counts_ref[...] > 1
    code = jnp.where(wanted, source, -1)
    rank = jnp.zeros(shape, jnp.int32)
    for head in range(head_total - 1):
        same = (code[:, head : head + 1] == source) & (of_head > head)
        rank = rank + same.astype(jnp.int32)
    first = wanted & (rank == 0)
    second = wanted & (rank == 1)
    further = wanted & (rank > 1)

    def along(block):
        total = jnp.sum(block.astype(jnp.float32), axis=1, keepdims=True)
        return jnp.broadcast_to(total.astype(jnp.int32), shape)

    def least_of_all(block):
        rows = jnp.min(block.astype(jnp.float32), axis=1, keepdims=True)
        lowest = jnp.min(rows, axis=0, keepdims=True)
        return jnp.broadcast_to(lowest.astype(jnp.int32), shape)

    def over_tiles(reduce, block):
        return jnp.broadcast_to(reduce(block, axis=0, keepdims=True), shape)

    bit = jnp.int32(1) << source
    mine = source == me
    none = 1 << 20
    tile_bits, head_bits = index_bits(tiles), index_bits(head_total)
    key = (((of_tile << head_bits) | of_head) << tile_bits) | source
    taken = along(jnp.where(first, bit, 0))
    state = (
        jnp.where(further, key, none),
        first.astype(jnp.int32),
        taken,
        taken,
        along(jnp.where(second, bit, 0)),
        along(jnp.where(first & mine, of_head, 0)),
        along(jnp.where(second & mine, of_head, 0)),
        jnp.where(first, source, jnp.where(second, tiles + source, 0)),
        jnp.zeros(shape, jnp.int32),
    )

    def relay(_, state):
        key, direct, held1, movable, held2, send1, send2, where, fail = state
        lowest = least_of_all(key)
        here = key == lowest
        start = lowest & ((1 << tile_bits) - 1)
        head = (lowest >> tile_bits) & ((1 << head_bits) - 1)
        to = lowest >> (tile_bits + head_bits)
        held2_to = over_tiles(jnp.max, jnp.where(of_tile == to, held2, 0))
        used1 = (held1 >> start) & 1
        fixed = 1 - ((movable >> start) & 1) * (1 - ((held2 >> start) & 1))
        free = ((held2_to >> of_tile) & 1) == 0
        free = free & (of_tile != start) & (of_tile != to) & ((used1 == 0) | (fixed == 0))
        best = over_tiles(jnp.min, jnp.where(free, of_tile + tiles * used1, none))
        good = best < none
        moved = good & (best >= tiles)
        via = jnp.where(good, jnp.where(moved, best - tiles, best), 0)
        at_via = good & (of_tile == via)
        at_to = good & (of_tile == to)
        shifted = at_via & moved & (direct > 0) & (source == start)
        where = jnp.where(shifted, tiles + start, where)
        where = jnp.where(here & good, tiles + via, where)
        direct = jnp.where(shifted, 0, direct)
        send2 = jnp.where(at_via & moved & (start == me), send1, send2)
        send1 = jnp.where(at_via & (start == me), head, send1)
        send2 = jnp.where(at_to & (via == me), head_total + start, send2)
        start_bit = jnp.int32(1) << start
        held1 = jnp.where(at_via, held1 | start_bit, held1)
        movable = jnp.where(at_via, movable & ~start_bit, movable)
        held2 = jnp.where(at_via & moved, held2 | start_bit, held2)
        held2 = jnp.where(at_to, held2 | (jnp.int32(1) << via), held2)
        fail = jnp.where(good, fail, 1)
        key = jnp.where(here, none, key)
        return key, direct, held1, movable, held2, send1, send2, where, fail

    relays = jnp.sum(further.astype(jnp.float32)).astype(jnp.int32)
    state = lax.fori_loop(0, relays, relay, state)
    send1, send2, where, fail = state[5:]
    route_ref[0] = send2
    route_ref[1] = where
    fail_ref[...] = fail
    sent = [pick_one(send1, of_tile == tile) for tile in range(tiles)]
    if STAGGER_NS:
        @pl.when(lax.axis_index("clip") % 2 == 1)
        def _():
            pl.delay(STAGGER_NS)

    all_read.wait()
    writes = [
        pltpu.make_async_copy(own_ref.at[sent[tile]], send_ref.at[tile], sems.at[1])
        for tile in range(tiles)
    ]
    for write in writes:
        write.start()
    pltpu.make_async_copy(own_ref.at[pl.ds(0, tiles)], send_ref, sems.at[1]).wait()


def pick_one(block, at):
    return jnp.max(jnp.where(at, block, 0), axis=0, keepdims=True)[0, 0]


def forward_kernel(route_ref, own_ref, got_ref, send_ref):
    tiles = send_ref.shape[0]
    head_total = own_ref.shape[0]
    route = route_ref[0]
    of_tile = lax.broadcasted_iota(jnp.int32, route.shape, 0)
    codes = [pick_one(route, of_tile == tile) for tile in range(tiles)]
    for tile, code in enumerate(codes):

        @pl.when(code < head_total)
        def _():
            send_ref[tile] = own_ref[code]

        @pl.when(code >= head_total)
        def _():
            send_ref[tile] = got_ref[code - head_total]


def route_attend_kernel(
    counts_ref, route_ref, query_ref, own_ref, got_ref, more_ref, out_ref, scores, weights
):
    tiles = got_ref.shape[0]
    where = jnp.broadcast_to(route_ref[1, pl.ds(position(), 1), :], route_ref.shape[1:])
    codes = [where[0, head] for head in range(where.shape[1])]

    def far(head, which):
        code = codes[head]
        at = lax.rem(code, tiles)
        return jnp.where(code < tiles, got_ref[at, which], more_ref[at, which])

    attend(
        counts_ref,
        query_ref,
        lambda head: own_ref[head, 0],
        lambda head: own_ref[head, 1],
        lambda head: far(head, 0),
        lambda head: far(head, 1),
        out_ref,
        scores,
        weights,
    )


def attend_by_owner_kernel(
    counts_ref, query_ref, key_ref, value_ref, far_ref, out_ref, scores, weights
):
    inner = far_ref.shape[1] // 2
    attend(
        counts_ref,
        query_ref,
        lambda head: key_ref[:, head * DH : (head + 1) * DH],
        lambda head: value_ref[:, head * DH : (head + 1) * DH],
        lambda head: far_ref[head // inner, 2 * (head % inner)],
        lambda head: far_ref[head // inner, 2 * (head % inner) + 1],
        out_ref,
        scores,
        weights,
    )


def shards_by_route(query_states, key_states, value_states, tile_lists, tile_counts):
    rows, width = query_states.shape
    tiles = lax.axis_size(GROUP)
    head_total = width // DH
    dtype = key_states.dtype
    block = jax.ShapeDtypeStruct((tiles, 2, rows, DH), dtype)
    send, own, route, fail = pl.pallas_call(
        plan_kernel,
        out_shape=[
            block,
            jax.ShapeDtypeStruct((head_total, 2, rows, DH), dtype),
            jax.ShapeDtypeStruct((2, tiles, head_total), jnp.int32),
            jax.ShapeDtypeStruct((tiles, head_total), jnp.int32),
        ],
        in_specs=[ANY] * 4,
        out_specs=[ANY] + [VMEM] * 3,
        scratch_shapes=[
            pltpu.VMEM((tiles, 2, head_total), jnp.int32),
            pltpu.VMEM((tiles, head_total), jnp.int32),
            pltpu.SemaphoreType.DMA((2,)),
            pltpu.SemaphoreType.DMA((2,)),
        ],
        compiler_params=PARAMS,
        name="plan",
    )(
        *(
            pltpu.with_memory_space_constraint(x, pltpu.HBM)
            for x in (tile_lists.transpose(1, 2, 0), tile_counts.T, key_states, value_states)
        )
    )
    got = lax.all_to_all(send, GROUP, split_axis=0, concat_axis=0, tiled=True)

    def routed(operands):
        query, _, _, _, counts, own, route, got = operands
        send = pl.pallas_call(
            forward_kernel,
            out_shape=block,
            in_specs=[VMEM] * 3,
            out_specs=VMEM,
            compiler_params=PARAMS,
            name="forward",
        )(route, own, got)
        more = lax.all_to_all(send, GROUP, split_axis=0, concat_axis=0, tiled=True)
        return pl.pallas_call(
            route_attend_kernel,
            out_shape=pltpu.HBM((rows, width), query.dtype),
            in_specs=[VMEM] * 6,
            out_specs=VMEM,
            scratch_shapes=attend_scratch(rows, width),
            compiler_params=PARAMS,
            name="attend",
        )(counts.T, route, query, own, got, more)

    def by_owner(operands):
        return shards_by_owner(*operands[:5])

    operands = (query_states, key_states, value_states, tile_lists, tile_counts, own, route, got)
    return lax.cond(fail[0, 0] > 0, by_owner, routed, operands)


def shards(query_states, key_states, value_states, tile_lists, tile_counts):
    rows = query_states.shape[0]
    head_total, tile_total, slots = tile_lists.shape
    owners = lax.axis_size(GROUP)
    one_tile = rows == TILE and tile_total == owners
    joins = tile_total * index_bits(tile_total) <= 24
    if one_tile and joins and slots == 2 and head_total % owners == 0:
        return shards_by_route(query_states, key_states, value_states, tile_lists, tile_counts)
    return shards_by_seq(query_states, key_states, value_states, tile_lists, tile_counts)


def solution(mesh):
    placed = (
        P(("clip", "seq", "help"), None),
        P(("clip", "seq", "help"), None),
        P(("clip", "seq", "help"), None),
        P("clip", None, None),
        P("clip", None),
    )
    return jax.shard_map(
        shards,
        mesh=mesh,
        in_specs=placed,
        out_specs=P(("clip", "seq", "help"), None),
        check_vma=False,
    )
```

```python
import math

import jax
import jax.numpy as jnp
from jax import lax
from jax.experimental import pallas as pl
from jax.experimental.pallas import tpu as pltpu
from jax.sharding import PartitionSpec as P

H = 16
DH = 128
TILE = 128
ROUND = 4


big_negative = -1e30


def pick_tiles(table, index):
    table_rows = table.shape[0]
    selector = (index[:, None] == jnp.arange(table_rows, dtype=jnp.int32)[None, :]).astype(
        jnp.bfloat16
    )
    picked = jnp.dot(selector, table.reshape(table_rows, -1), preferred_element_type=jnp.float32)
    return picked.astype(jnp.bfloat16).reshape((index.shape[0],) + table.shape[1:])


def attend_items(query_items, key_tiles, value_tiles, item_lists, item_counts):
    item_total, tile_rows, head_width = query_items.shape
    factor = head_width ** (-0.5)
    batches = item_total // ROUND
    joined = jnp.concatenate((key_tiles, value_tiles), axis=2)

    def one_batch(packed):
        queries, lists, counts = packed
        start_state = (
            jnp.full((ROUND, tile_rows, 1), big_negative, jnp.float32),
            jnp.zeros((ROUND, tile_rows, 1), jnp.float32),
            jnp.zeros((ROUND, tile_rows, head_width), jnp.float32),
        )

        def one_slot(slot_index, carried):
            running_max, running_sum, weighted = carried
            chosen = lax.dynamic_index_in_dim(lists, slot_index, axis=1, keepdims=False)
            both_blocks = pick_tiles(joined, chosen)
            key_block = both_blocks[:, :, :head_width]
            value_block = both_blocks[:, :, head_width:]
            scores = (
                jnp.einsum("qtd,qsd->qts", queries, key_block, preferred_element_type=jnp.float32)
                * factor
            )
            new_max = jnp.maximum(running_max, jnp.max(scores, axis=2, keepdims=True))
            shrink = jnp.exp(running_max - new_max)
            tile_weights = jnp.exp(scores - new_max)
            new_sum = running_sum * shrink + jnp.sum(tile_weights, axis=2, keepdims=True)
            new_weighted = weighted * shrink + jnp.einsum(
                "qts,qsd->qtd",
                tile_weights.astype(jnp.bfloat16),
                value_block,
                preferred_element_type=jnp.float32,
            )
            live = (slot_index < counts)[:, None, None]
            return (
                jnp.where(live, new_max, running_max),
                jnp.where(live, new_sum, running_sum),
                jnp.where(live, new_weighted, weighted),
            )

        final_state = lax.fori_loop(0, jnp.max(counts), one_slot, start_state)
        return (final_state[2] / final_state[1]).astype(jnp.bfloat16)

    finished = lax.map(
        one_batch,
        (
            query_items.reshape(batches, ROUND, tile_rows, head_width),
            item_lists.reshape(batches, ROUND, item_lists.shape[1]),
            item_counts.reshape(batches, ROUND),
        ),
    )
    return finished.reshape(item_total, tile_rows, head_width)


def shards_by_seq(query_states, key_states, value_states, tile_lists, tile_counts):
    groups = lax.axis_size("seq")
    helpers = lax.axis_size("help")
    device = lax.axis_index("seq")
    helper = lax.axis_index("help")
    row_count = query_states.shape[0]
    heads_here = H // groups
    head_cols = heads_here * DH
    tile_total = tile_lists.shape[1]
    per_block = row_count // TILE
    owned_total = groups * per_block

    def to_groups(states):
        return states.reshape(row_count, groups, head_cols)

    arrived = (
        lax.all_to_all(to_groups(query_states), "seq", split_axis=1, concat_axis=0, tiled=True),
        lax.all_to_all(to_groups(key_states), "seq", split_axis=1, concat_axis=0, tiled=True),
        lax.all_to_all(to_groups(value_states), "seq", split_axis=1, concat_axis=0, tiled=True),
    )
    arrived_query = arrived[0].reshape(groups, 1, row_count, head_cols)
    arrived_key = arrived[1].reshape(groups, 1, row_count, head_cols)
    arrived_value = arrived[2].reshape(groups, 1, row_count, head_cols)
    head_lists = lax.dynamic_slice_in_dim(tile_lists, device * heads_here, heads_here, 0)
    head_counts = lax.dynamic_slice_in_dim(tile_counts, device * heads_here, heads_here, 0)
    head_offset = (jnp.arange(heads_here, dtype=jnp.int32) * tile_total)[:, None, None]
    flat_lists = (head_lists + head_offset).reshape(heads_here * tile_total, head_lists.shape[2])
    flat_counts = head_counts.reshape(heads_here * tile_total)

    def head_tiles(whole):
        shaped = whole.reshape(tile_total, TILE, heads_here, DH).transpose(2, 0, 1, 3)
        return shaped.reshape(heads_here * tile_total, TILE, DH)

    key_whole, value_whole = (
        lax.all_gather(arrived_key, "help", axis=1, tiled=True),
        lax.all_gather(arrived_value, "help", axis=1, tiled=True),
    )
    key_tiles = head_tiles(key_whole)
    value_tiles = head_tiles(value_whole)
    own_tiles = arrived_query.reshape(owned_total, TILE, heads_here, DH).transpose(2, 0, 1, 3)
    own_tiles = own_tiles.reshape(heads_here * owned_total, TILE, DH)
    local_index = jnp.arange(owned_total, dtype=jnp.int32)
    global_tile = (
        local_index // per_block * helpers + helper
    ) * per_block + local_index % per_block
    item_index = (
        jnp.arange(heads_here, dtype=jnp.int32)[:, None] * tile_total + global_tile[None, :]
    )
    item_index = item_index.reshape(heads_here * owned_total)
    results = attend_items(
        own_tiles,
        key_tiles,
        value_tiles,
        jnp.take(flat_lists, item_index, axis=0),
        jnp.take(flat_counts, item_index, axis=0),
    )
    owned = results.reshape(heads_here, owned_total, TILE, DH)
    leaving = owned.transpose(1, 2, 0, 3)
    leaving = leaving.reshape(groups, row_count, head_cols)
    returned = lax.all_to_all(leaving, "seq", split_axis=0, concat_axis=2, tiled=True)
    return returned.reshape(row_count, H * DH)


GROUP = ("seq", "help")
ANY = pl.BlockSpec(memory_space=pl.ANY)
VMEM = pl.BlockSpec(memory_space=pltpu.VMEM)
PARAMS = pltpu.CompilerParams(vmem_limit_bytes=12 << 20)
STAGGER_NS = 8000


def position():
    return lax.axis_index("seq") * lax.axis_size("help") + lax.axis_index("help")


def pack_kernel(key_ref, value_ref, out_ref, sems):
    owners, parts = out_ref.shape[:2]
    reads = []
    for owner in range(owners):
        for part in range(parts):
            source = (key_ref, value_ref)[part % 2]
            head = owner * (parts // 2) + part // 2
            reads.append(
                pltpu.make_async_copy(
                    source.at[:, head * DH : (head + 1) * DH],
                    out_ref.at[owner, part],
                    sems.at[owner * parts + part],
                )
            )
            reads[-1].start()
    for read in reads:
        read.wait()


def index_bits(tiles):
    return (tiles - 1).bit_length()


def pick_kernel(lists_ref, held_ref, out_ref):
    tiles, parts = out_ref.shape[:2]
    heads = parts // 2
    bits = index_bits(tiles)
    first = position() * heads
    listed = lists_ref[:, 1, :]
    of_head = lax.broadcasted_iota(jnp.int32, listed.shape, 1)
    of_tile = lax.broadcasted_iota(jnp.int32, listed.shape, 0)
    placed = listed << (bits * of_tile)
    for head in range(heads):
        own = jnp.where(of_head == first + head, placed, 0).astype(jnp.float32)
        joined = jnp.sum(own).astype(jnp.int32)
        pair = slice(2 * head, 2 * head + 2)
        for tile in range(tiles):
            chosen = (joined >> (bits * tile)) & ((1 << bits) - 1)
            out_ref[tile, pair] = held_ref[chosen, pair]


def attend(counts_ref, query_ref, key, value, far_key, far_value, out_ref, scores, weights):
    width = query_ref.shape[1]
    factor = DH ** (-0.5) * math.log2(math.e)
    heads = width // DH
    counts = counts_ref[pl.ds(position(), 1), :]
    square = (counts.shape[1], counts.shape[1])
    own = lax.broadcasted_iota(jnp.int32, square, 0) == lax.broadcasted_iota(jnp.int32, square, 1)
    used = jnp.sum(jnp.where(own, counts, 0).astype(jnp.float32), axis=1, keepdims=True) > 1.5
    masks = jnp.where(jnp.broadcast_to(used, (square[0], TILE)), 0.0, big_negative)

    def score(head):
        scores[head] = lax.dot_general(
            query_ref[:, head * DH : (head + 1) * DH],
            jnp.concatenate((key(head), far_key(head)), axis=0),
            (((1,), (1,)), ((), ())),
            preferred_element_type=jnp.float32,
        )

    def weigh(head):
        near = scores[head, :, :TILE]
        far = scores[head, :, TILE:] + masks[head : head + 1]
        top = jnp.max(jnp.maximum(near, far), axis=1, keepdims=True)
        weights[head, :, :TILE] = jnp.exp2((near - top) * factor).astype(weights.dtype)
        weights[head, :, TILE:] = jnp.exp2((far - top) * factor).astype(weights.dtype)

    def gather(head):
        values = jnp.concatenate((value(head), far_value(head)), axis=0)
        widened = jnp.concatenate((values, jnp.ones_like(values)), axis=1)
        product = jnp.dot(weights[head], widened, preferred_element_type=jnp.float32)
        out_ref[:, head * DH : (head + 1) * DH] = (product[:, :DH] / product[:, DH:]).astype(
            out_ref.dtype
        )

    stages = ((0, score), (1, weigh), (2, gather))
    for step in range(heads + stages[-1][0]):
        for lag, stage in stages:
            if 0 <= step - lag < heads:
                stage(step - lag)


def attend_scratch(rows, width):
    shape = (width // DH, rows, 2 * TILE)
    return [pltpu.VMEM(shape, jnp.float32), pltpu.VMEM(shape, jnp.bfloat16)]


def shards_by_owner(query_states, key_states, value_states, tile_lists, tile_counts):
    rows, width = query_states.shape
    owners = lax.axis_size(GROUP)
    parts = 2 * width // DH // owners
    block = jax.ShapeDtypeStruct((owners, parts, rows, DH), key_states.dtype)
    packed = pl.pallas_call(
        pack_kernel,
        out_shape=block,
        in_specs=[ANY, ANY],
        out_specs=VMEM,
        scratch_shapes=[pltpu.SemaphoreType.DMA((owners * parts,))],
        compiler_params=PARAMS,
        name="pack",
    )(*(pltpu.with_memory_space_constraint(x, pltpu.HBM) for x in (key_states, value_states)))
    held = lax.all_to_all(packed, GROUP, split_axis=0, concat_axis=0, tiled=True)
    picked = pl.pallas_call(
        pick_kernel,
        out_shape=block,
        in_specs=[VMEM, VMEM],
        out_specs=VMEM,
        compiler_params=PARAMS,
        name="pick",
    )(tile_lists.transpose(1, 2, 0), held)
    far = lax.all_to_all(picked, GROUP, split_axis=0, concat_axis=0, tiled=True)
    return pl.pallas_call(
        attend_by_owner_kernel,
        out_shape=pltpu.HBM((rows, width), query_states.dtype),
        in_specs=[VMEM] * 5,
        out_specs=VMEM,
        scratch_shapes=attend_scratch(rows, width),
        compiler_params=PARAMS,
        name="attend",
    )(tile_counts.T, query_states, key_states, value_states, far)


def plan_kernel(
    lists_source,
    counts_source,
    key_ref,
    value_ref,
    send_ref,
    own_ref,
    route_ref,
    fail_ref,
    lists_ref,
    counts_ref,
    sems,
    table_sems,
):
    tiles, head_total = counts_ref.shape
    tables = [
        pltpu.make_async_copy(lists_source, lists_ref, table_sems.at[0]),
        pltpu.make_async_copy(counts_source, counts_ref, table_sems.at[1]),
    ]
    for table in tables:
        table.start()
    for which, source in enumerate((key_ref, value_ref)):
        pltpu.make_async_copy(source, own_ref.at[which], sems.at[0]).start()
    all_read = pltpu.make_async_copy(own_ref, own_ref, sems.at[0])

    me = position()
    shape = (tiles, head_total)
    of_tile = lax.broadcasted_iota(jnp.int32, shape, 0)
    of_head = lax.broadcasted_iota(jnp.int32, shape, 1)
    for table in tables:
        table.wait()
    source = lists_ref[:, 1, :]
    wanted = counts_ref[...] > 1
    code = jnp.where(wanted, source, -1)
    rank = jnp.zeros(shape, jnp.int32)
    for head in range(head_total - 1):
        same = (code[:, head : head + 1] == source) & (of_head > head)
        rank = rank + same.astype(jnp.int32)
    first = wanted & (rank == 0)
    second = wanted & (rank == 1)
    further = wanted & (rank > 1)

    def along(block):
        total = jnp.sum(block.astype(jnp.float32), axis=1, keepdims=True)
        return jnp.broadcast_to(total.astype(jnp.int32), shape)

    def least_of_all(block):
        rows = jnp.min(block.astype(jnp.float32), axis=1, keepdims=True)
        lowest = jnp.min(rows, axis=0, keepdims=True)
        return jnp.broadcast_to(lowest.astype(jnp.int32), shape)

    def over_tiles(reduce, block):
        return jnp.broadcast_to(reduce(block, axis=0, keepdims=True), shape)

    bit = jnp.int32(1) << source
    mine = source == me
    none = 1 << 20
    tile_bits, head_bits = index_bits(tiles), index_bits(head_total)
    key = (((of_tile << head_bits) | of_head) << tile_bits) | source
    taken = along(jnp.where(first, bit, 0))
    state = (
        jnp.where(further, key, none),
        first.astype(jnp.int32),
        taken,
        taken,
        along(jnp.where(second, bit, 0)),
        along(jnp.where(first & mine, of_head, 0)),
        along(jnp.where(second & mine, of_head, 0)),
        jnp.where(first, source, jnp.where(second, tiles + source, 0)),
        jnp.zeros(shape, jnp.int32),
    )

    def relay(_, state):
        key, direct, held1, movable, held2, send1, send2, where, fail = state
        lowest = least_of_all(key)
        here = key == lowest
        start = lowest & ((1 << tile_bits) - 1)
        head = (lowest >> tile_bits) & ((1 << head_bits) - 1)
        to = lowest >> (tile_bits + head_bits)
        held2_to = over_tiles(jnp.max, jnp.where(of_tile == to, held2, 0))
        used1 = (held1 >> start) & 1
        fixed = 1 - ((movable >> start) & 1) * (1 - ((held2 >> start) & 1))
        free = ((held2_to >> of_tile) & 1) == 0
        free = free & (of_tile != start) & (of_tile != to) & ((used1 == 0) | (fixed == 0))
        best = over_tiles(jnp.min, jnp.where(free, of_tile + tiles * used1, none))
        good = best < none
        moved = good & (best >= tiles)
        via = jnp.where(good, jnp.where(moved, best - tiles, best), 0)
        at_via = good & (of_tile == via)
        at_to = good & (of_tile == to)
        shifted = at_via & moved & (direct > 0) & (source == start)
        where = jnp.where(shifted, tiles + start, where)
        where = jnp.where(here & good, tiles + via, where)
        direct = jnp.where(shifted, 0, direct)
        send2 = jnp.where(at_via & moved & (start == me), send1, send2)
        send1 = jnp.where(at_via & (start == me), head, send1)
        send2 = jnp.where(at_to & (via == me), head_total + start, send2)
        start_bit = jnp.int32(1) << start
        held1 = jnp.where(at_via, held1 | start_bit, held1)
        movable = jnp.where(at_via, movable & ~start_bit, movable)
        held2 = jnp.where(at_via & moved, held2 | start_bit, held2)
        held2 = jnp.where(at_to, held2 | (jnp.int32(1) << via), held2)
        fail = jnp.where(good, fail, 1)
        key = jnp.where(here, none, key)
        return key, direct, held1, movable, held2, send1, send2, where, fail

    relays = jnp.sum(further.astype(jnp.float32)).astype(jnp.int32)
    state = lax.fori_loop(0, relays, relay, state)
    send1, send2, where, fail = state[5:]
    route_ref[0] = send2
    route_ref[1] = where
    fail_ref[...] = fail
    sent = [pick_one(send1, of_tile == tile) for tile in range(tiles)]
    if STAGGER_NS:
        @pl.when(lax.axis_index("clip") % 2 == 1)
        def _():
            pl.delay(STAGGER_NS)

    all_read.wait()
    for tile in range(tiles):
        for which in range(2):
            pltpu.make_async_copy(
                own_ref.at[which, :, columns(sent[tile])], send_ref.at[tile, which], sems.at[1]
            ).start()
    pltpu.make_async_copy(send_ref, send_ref, sems.at[1]).wait()


def columns(head):
    return pl.ds(pl.multiple_of(head * DH, DH), DH)


def pick_one(block, at):
    return jnp.max(jnp.where(at, block, 0), axis=0, keepdims=True)[0, 0]


def forward_kernel(route_ref, own_ref, got_ref, send_ref):
    tiles = send_ref.shape[0]
    head_total = own_ref.shape[2] // DH
    route = route_ref[0]
    of_tile = lax.broadcasted_iota(jnp.int32, route.shape, 0)
    codes = [pick_one(route, of_tile == tile) for tile in range(tiles)]
    for tile, code in enumerate(codes):

        @pl.when(code < head_total)
        def _():
            for which in range(2):
                send_ref[tile, which] = own_ref[which, :, columns(code)]

        @pl.when(code >= head_total)
        def _():
            send_ref[tile] = got_ref[code - head_total]


def route_attend_kernel(
    counts_ref, route_ref, query_ref, own_ref, got_ref, more_ref, out_ref, scores, weights
):
    tiles = got_ref.shape[0]
    where = jnp.broadcast_to(route_ref[1, pl.ds(position(), 1), :], route_ref.shape[1:])
    codes = [where[0, head] for head in range(where.shape[1])]

    def far(head, which):
        code = codes[head]
        at = lax.rem(code, tiles)
        return jnp.where(code < tiles, got_ref[at, which], more_ref[at, which])

    attend(
        counts_ref,
        query_ref,
        lambda head: own_ref[0, :, head * DH : (head + 1) * DH],
        lambda head: own_ref[1, :, head * DH : (head + 1) * DH],
        lambda head: far(head, 0),
        lambda head: far(head, 1),
        out_ref,
        scores,
        weights,
    )


def attend_by_owner_kernel(
    counts_ref, query_ref, key_ref, value_ref, far_ref, out_ref, scores, weights
):
    inner = far_ref.shape[1] // 2
    attend(
        counts_ref,
        query_ref,
        lambda head: key_ref[:, head * DH : (head + 1) * DH],
        lambda head: value_ref[:, head * DH : (head + 1) * DH],
        lambda head: far_ref[head // inner, 2 * (head % inner)],
        lambda head: far_ref[head // inner, 2 * (head % inner) + 1],
        out_ref,
        scores,
        weights,
    )


def shards_by_route(query_states, key_states, value_states, tile_lists, tile_counts):
    rows, width = query_states.shape
    tiles = lax.axis_size(GROUP)
    head_total = width // DH
    dtype = key_states.dtype
    block = jax.ShapeDtypeStruct((tiles, 2, rows, DH), dtype)
    send, own, route, fail = pl.pallas_call(
        plan_kernel,
        out_shape=[
            block,
            jax.ShapeDtypeStruct((2, rows, width), dtype),
            jax.ShapeDtypeStruct((2, tiles, head_total), jnp.int32),
            jax.ShapeDtypeStruct((tiles, head_total), jnp.int32),
        ],
        in_specs=[ANY] * 4,
        out_specs=[ANY] + [VMEM] * 3,
        scratch_shapes=[
            pltpu.VMEM((tiles, 2, head_total), jnp.int32),
            pltpu.VMEM((tiles, head_total), jnp.int32),
            pltpu.SemaphoreType.DMA((2,)),
            pltpu.SemaphoreType.DMA((2,)),
        ],
        compiler_params=PARAMS,
        name="plan",
    )(
        *(
            pltpu.with_memory_space_constraint(x, pltpu.HBM)
            for x in (tile_lists.transpose(1, 2, 0), tile_counts.T, key_states, value_states)
        )
    )
    got = lax.all_to_all(send, GROUP, split_axis=0, concat_axis=0, tiled=True)

    def routed(operands):
        query, _, _, _, counts, own, route, got = operands
        send = pl.pallas_call(
            forward_kernel,
            out_shape=block,
            in_specs=[VMEM] * 3,
            out_specs=VMEM,
            compiler_params=PARAMS,
            name="forward",
        )(route, own, got)
        more = lax.all_to_all(send, GROUP, split_axis=0, concat_axis=0, tiled=True)
        return pl.pallas_call(
            route_attend_kernel,
            out_shape=pltpu.HBM((rows, width), query.dtype),
            in_specs=[VMEM] * 6,
            out_specs=VMEM,
            scratch_shapes=attend_scratch(rows, width),
            compiler_params=PARAMS,
            name="attend",
        )(counts.T, route, query, own, got, more)

    def by_owner(operands):
        return shards_by_owner(*operands[:5])

    operands = (query_states, key_states, value_states, tile_lists, tile_counts, own, route, got)
    return lax.cond(fail[0, 0] > 0, by_owner, routed, operands)


def shards(query_states, key_states, value_states, tile_lists, tile_counts):
    rows = query_states.shape[0]
    head_total, tile_total, slots = tile_lists.shape
    owners = lax.axis_size(GROUP)
    one_tile = rows == TILE and tile_total == owners
    joins = tile_total * index_bits(tile_total) <= 24
    if one_tile and joins and slots == 2 and head_total % owners == 0:
        return shards_by_route(query_states, key_states, value_states, tile_lists, tile_counts)
    return shards_by_seq(query_states, key_states, value_states, tile_lists, tile_counts)


def solution(mesh):
    placed = (
        P(("clip", "seq", "help"), None),
        P(("clip", "seq", "help"), None),
        P(("clip", "seq", "help"), None),
        P("clip", None, None),
        P("clip", None),
    )
    return jax.shard_map(
        shards,
        mesh=mesh,
        in_specs=placed,
        out_specs=P(("clip", "seq", "help"), None),
        check_vma=False,
    )
```
